256 devices in a mesh: win: 16 (over x_hi, y, core), blk: 16 (over x_lo, z).
Axes of the slice: x: 4 (x_hi: 2, x_lo: 2; x = x_hi * 2 + x_lo), y: 4, z: 8, core: 2. Of those that a mesh axis runs over, the one named last changes fastest.
Arguments:
- sample: float32 [512, 16, 8, 128], P(('win', 'blk')), parts along dimension 0, may hold values from -6 to 6
- fresh_noise: float32 [512, 16, 8, 128], P(('win', 'blk')), parts along dimension 0, may hold values from -6 to 6
- proxy_month: int32 [65536], P('win'), parts along dimension 0, may hold values from 0 to 31, as said below
- proxy_cell: int32 [65536], P('win'), parts along dimension 0, may hold values from 0 to 2047, as said below
- proxy_var: int32 [65536], P('win'), parts along dimension 0, may hold values from 0 to 7
- observed: float32 [65536], P('win'), parts along dimension 0, may hold values from -8 to 8
- proxy_weight: float32 [65536], P('win'), parts along dimension 0, may hold values from 0.25 to 4
- lift_weight: bfloat16 [64, 8], replicated, may hold values from -2 to 2
- month_kernels: bfloat16 [2, 3, 64, 64], replicated, may hold values from -0.4375 to 0.4375
- grid_kernels: bfloat16 [2, 3, 3, 64, 64], replicated, may hold values from -0.25 to 0.25
- read_weight: bfloat16 [8, 64], replicated, may hold values from -0.75 to 0.75
Outputs:
- updated: float32 [512, 16, 8, 128], P(('win', 'blk')), parts along dimension 0
The draws below stay inside these ranges and needn't reach their ends.
There are 16 independent parts, one for each index of `win`. The reference program is written for one: setup_inputs(seed, part) draws one part's arguments, and reference() takes and returns one part's arrays. A program takes and returns all parts, laid end to end along the dimension named above; an argument that names none is the same for every part. Nothing has to cross between parts.
Inputs may be any that keep to these rules, and one draw needn't show every extreme that they name: `proxy_month`: several observations may fall on the same cell, month and variable. `proxy_cell`: A cell is its latitude row times 128 plus its longitude cell.
All inputs are finite; a program needn't handle non-finite values.
Results may differ from the reference program's by a relative error of at most 0.0035.
Values may be sent and summed in bfloat16 or wider, within the bound.
A program may use at most 64 MiB of HBM per device.

```python
import math
import jax
import jax.numpy as jnp
from jax import lax

C = 64
V = 8
LON = 128
LAT = 16
TM = 32
NPROX = 4096


def draw_proxy_month(key, part):
    mixture = jax.random.randint(jax.random.fold_in(key, 11), (NPROX,), 0, 2)
    uniform_month = jax.random.randint(jax.random.fold_in(key, 12), (NPROX,), 0, TM)
    later_month = jax.random.randint(jax.random.fold_in(key, 13), (NPROX,), 0, TM)
    months = jnp.where(mixture == 0, uniform_month, jnp.maximum(uniform_month, later_month))
    return months.at[0].set(0).at[1].set(TM - 1).astype(jnp.int32)


def draw_proxy_cell(key, part):
    cells = jax.random.randint(jax.random.fold_in(key, 21), (NPROX,), 0, LAT * LON)
    return cells.at[0].set(0).at[1].set(LAT * LON - 1).astype(jnp.int32)


def touch_ends(entries, stream_key, least, top_value):
    shape = entries.shape
    index_at = [jax.random.randint(jax.random.fold_in(stream_key, axis), (), 0, shape[axis]) for axis in range(len(shape))]
    entries = entries.at[tuple(index_at)].set(least)
    longest = shape.index(max(shape))
    index_at[longest] = (index_at[longest] + 1) % shape[longest]
    return entries.at[tuple(index_at)].set(top_value)


def shard_levels(rng, shape, pieces, low, largest):
    loudness, own = 1.0, jax.random.fold_in(rng, 6)
    for axis_at, shards_of in pieces:
        draws = jnp.exp(jax.random.uniform(jax.random.fold_in(own, axis_at), (shards_of,), jnp.float32, low / len(pieces), largest / len(pieces)))
        loudness = loudness * jnp.repeat(draws, shape[axis_at] // shards_of).reshape([-1 if axis == axis_at else 1 for axis in range(len(shape))])
    return loudness


def noise(key, extent, deviation, reach, split=(), dtype=jnp.bfloat16):
    gain = shard_levels(key, extent, split, -0.22, 0.18) if split else 1.0
    result = jax.random.normal(key, extent, jnp.float32) * deviation * gain
    return jnp.minimum(jnp.maximum(result, -reach), reach).astype(dtype)


def setup_inputs(seed: int = 0, part: int = 0) -> dict:
    seeds = jax.random.split(jax.random.key(seed), 12)
    own_keys = jax.random.split(jax.random.fold_in(seeds[11], part), 12)
    return {
        "sample": noise(own_keys[0], (TM, LAT, V, LON), 1.0, 6.0, ((0, 16),), jnp.float32),
        "fresh_noise": noise(own_keys[1], (TM, LAT, V, LON), 1.0, 6.0, ((0, 16),), jnp.float32),
        "proxy_month": draw_proxy_month(jax.random.fold_in(jax.random.fold_in(seeds[11], part), 71), part),
        "proxy_cell": draw_proxy_cell(jax.random.fold_in(jax.random.fold_in(seeds[11], part), 71), part),
        "proxy_var": touch_ends(jax.random.randint(own_keys[4], (NPROX,), 0, V), jax.random.fold_in(own_keys[4], 1), 0, V - 1).astype(jnp.int32),
        "observed": noise(own_keys[5], (NPROX,), 1.5, 8.0, (), jnp.float32),
        "proxy_weight": jnp.clip(jnp.exp(jax.random.uniform(own_keys[6], (NPROX,), jnp.float32, math.log(0.25), math.log(4.0))), 0.25, 4.0),
        "lift_weight": noise(seeds[7], (C, V), V ** -0.5, 2.0),
        "month_kernels": noise(seeds[8], (2, 3, C, C), (3 * C) ** -0.5, 0.4375),
        "grid_kernels": noise(seeds[9], (2, 3, 3, C, C), (9 * C) ** -0.5, 0.25),
        "read_weight": noise(seeds[10], (V, C), C ** -0.5, 0.75),
    }


tweedie_gain = 0.5
step_size = 0.25
guide_gain = 4.0
noise_gain = 0.5 ** 0.5

def month_conv(source, kernels, dilation):
    months = source.shape[0]
    padded = jnp.pad(source.astype(jnp.float32), ((dilation, dilation), (0, 0), (0, 0), (0, 0)))
    summed = jnp.zeros(source.shape, jnp.float32)
    for offset in range(3):
        sliced = padded[offset * dilation:offset * dilation + months]
        summed = summed + jnp.einsum('dc,tlco->tldo', kernels[offset].astype(jnp.float32), sliced)
    return summed

def grid_conv(source, kernels):
    lat_rows = source.shape[1]
    lon_cells = source.shape[3]
    padded = jnp.pad(source.astype(jnp.float32), ((0, 0), (1, 1), (0, 0), (1, 1)))
    summed = jnp.zeros(source.shape, jnp.float32)
    for lat_shift in range(3):
        for lon_shift in range(3):
            sliced = padded[:, lat_shift:lat_shift + lat_rows, :, lon_shift:lon_shift + lon_cells]
            summed = summed + jnp.einsum('dc,tlco->tldo', kernels[lat_shift, lon_shift].astype(jnp.float32), sliced)
    return summed

def flip_months(kernels):
    return jnp.swapaxes(kernels[::-1], 1, 2)

def flip_grid(kernels):
    return jnp.swapaxes(kernels[::-1, ::-1], 2, 3)

def gelu_back(inner, cotangent):
    return jax.vjp(jax.nn.gelu, inner)[1](cotangent)[0]

def next_hidden(hidden, inner):
    return (hidden.astype(jnp.float32) + jax.nn.gelu(inner)).astype(jnp.bfloat16)

def back_step(adjoint, inner, kernels, dilation, temporal):
    scaled = gelu_back(inner, adjoint.astype(jnp.float32)).astype(jnp.bfloat16)
    if temporal:
        spread = month_conv(scaled, flip_months(kernels), dilation)
    else:
        spread = grid_conv(scaled, flip_grid(kernels))
    return (adjoint.astype(jnp.float32) + spread).astype(jnp.bfloat16)

def reference(sample, fresh_noise, proxy_month, proxy_cell, proxy_var, observed, proxy_weight, lift_weight, month_kernels, grid_kernels, read_weight):
    lat_rows = sample.shape[1]
    var_count = sample.shape[2]
    lon_cells = sample.shape[3]
    hidden_zero = jnp.einsum('cv,tlvo->tlco', lift_weight.astype(jnp.float32), sample, precision=lax.Precision.HIGHEST).astype(jnp.bfloat16)
    inner_one = month_conv(hidden_zero, month_kernels[0], 1)
    hidden_one = next_hidden(hidden_zero, inner_one)
    inner_two = month_conv(hidden_one, month_kernels[1], 2)
    hidden_two = next_hidden(hidden_one, inner_two)
    inner_three = grid_conv(hidden_two, grid_kernels[0])
    hidden_three = next_hidden(hidden_two, inner_three)
    inner_four = grid_conv(hidden_three, grid_kernels[1])
    hidden_four = next_hidden(hidden_three, inner_four)
    score = jnp.einsum('vc,tlco->tlvo', read_weight.astype(jnp.float32), hidden_four.astype(jnp.float32))
    denoised = sample + tweedie_gain * score
    flat_index = ((proxy_month * lat_rows + proxy_cell // lon_cells) * var_count + proxy_var) * lon_cells + proxy_cell % lon_cells
    flat_index = flat_index.astype(jnp.int32)
    misfit = denoised.reshape(-1)[flat_index] - observed
    misfit_norm = jnp.sqrt(jnp.mean(proxy_weight * misfit * misfit) + 1e-05)
    forcing = guide_gain * proxy_weight * misfit / misfit_norm
    adjoint_denoised = jnp.zeros((sample.size,), jnp.float32).at[flat_index].add(forcing).reshape(sample.shape)
    adjoint_four = jnp.einsum('vc,tlvo->tlco', read_weight.astype(jnp.float32), tweedie_gain * adjoint_denoised, precision=lax.Precision.HIGHEST).astype(jnp.bfloat16)
    adjoint_three = back_step(adjoint_four, inner_four, grid_kernels[1], 1, False)
    adjoint_two = back_step(adjoint_three, inner_three, grid_kernels[0], 1, False)
    adjoint_one = back_step(adjoint_two, inner_two, month_kernels[1], 2, True)
    adjoint_zero = back_step(adjoint_one, inner_one, month_kernels[0], 1, True)
    lifted_back = jnp.einsum('cv,tlco->tlvo', lift_weight.astype(jnp.float32), adjoint_zero.astype(jnp.float32))
    gradient = adjoint_denoised + lifted_back
    return sample + step_size * (score - gradient) + noise_gain * fresh_noise
```

```python
import functools

import jax
import jax.numpy as jnp
from jax import lax
from jax.experimental import pallas as pl
from jax.experimental.pallas import tpu as pltpu
from jax.sharding import PartitionSpec as P

tweedie_gain = 0.5
step_size = 0.25
guide_gain = 4.0
noise_gain = 0.5**0.5

f32 = jnp.float32
bf16 = jnp.bfloat16
MESH = pl.DeviceIdType.MESH

gelu_c = 0.7978845608028654
gelu_ca = gelu_c * 0.044715


def gelu_parts(x):
    x2 = x * x
    u = x * (gelu_c + gelu_ca * x2)
    h = 0.5 * jnp.tanh(u) + 0.5
    g = x * h
    dg = h + (g - g * h) * (2.0 * gelu_c + 6.0 * gelu_ca * x2)
    return g, dg


def dot(a, b):
    return jnp.dot(a, b, preferred_element_type=f32)


def dot_nt(a, b):
    return lax.dot_general(a, b, (((1,), (1,)), ((), ())), preferred_element_type=f32)


def lanes(*parts):
    return jnp.concatenate(parts, axis=1)


def rows(*parts):
    return jnp.concatenate(parts, axis=0)


def lon_sum(out, first, last):
    halves = []
    for m in range(2):
        cols = slice(128 * m, 128 * (m + 1))
        left = pltpu.roll(out[0:128, cols], 1, 1)
        right = pltpu.roll(out[256:384, cols], 127, 1)
        total = out[128:256, cols] + jnp.where(first, 0.0, left) + jnp.where(last, 0.0, right)
        halves.append(total)
    return lanes(*halves)


def grid_weights(block):
    zero = jnp.zeros((64, 64), f32)
    out = []
    for b in range(3):
        k0, k1, k2 = block(0, b), block(1, b), block(2, b)
        out.append(lanes(k0, k1, k2, zero))
        out.append(lanes(zero, k0, k1, k2))
    return rows(*out).astype(bf16)


def kernel(
    blk,
    sample_ref, noise_ref, month_ref, cell_ref, var_ref, obs_ref, pw_ref,
    lift_ref, mk_ref, gk_ref, read_ref,
    out_ref,
    send_pair, send_lo, send_hi, halo_l, halo_r, halo_ll, halo_rr,
    wf1, wf2, wf3, wf4, wb4, wb3, wb2, wb1, wread, wreadt,
    field,
    g1, g2, g3, g4, h2s, h3s, s4s, s3s, a4, a3,
    base, grad,
    gs_l, gs_r, gs_ll, gs_rr, gr_l, gr_r, gr_ll, gr_rr,
    psend, pbuf,
    hs_sem, hr_sem, gs_sem, gr_sem, ps_sem, pr_sem,
):
    me = lax.axis_index("blk")

    def peer(k):
        return lax.rem(me + k + blk, blk)

    def remote(src, dst, ssem, rsem, k):
        return pltpu.make_async_remote_copy(
            src_ref=src, dst_ref=dst, send_sem=ssem, recv_sem=rsem,
            device_id={"blk": peer(k)}, device_id_type=MESH,
        )

    barrier = pltpu.get_barrier_semaphore()
    for k in range(1, blk):
        pl.semaphore_signal(barrier, inc=1, device_id={"blk": peer(k)}, device_id_type=MESH)

    for l in range(16):
        send_pair[l] = rows(sample_ref[0, l], sample_ref[1, l]).astype(bf16)
    for q in range(8):
        send_lo[q] = rows(sample_ref[0, 2 * q], sample_ref[0, 2 * q + 1]).astype(bf16)
        send_hi[q] = rows(sample_ref[1, 2 * q], sample_ref[1, 2 * q + 1]).astype(bf16)

    pl.semaphore_wait(barrier, blk - 1)
    halo = [
        remote(send_pair, halo_l, hs_sem.at[0], hr_sem.at[0], 1),
        remote(send_pair, halo_r, hs_sem.at[1], hr_sem.at[1], -1),
        remote(send_hi, halo_ll, hs_sem.at[2], hr_sem.at[2], 2),
        remote(send_lo, halo_rr, hs_sem.at[3], hr_sem.at[3], -2),
    ]
    for copy in halo:
        copy.start()

    has_l = jnp.where(me > 0, 1.0, 0.0).astype(f32)
    has_ll = jnp.where(me > 1, 1.0, 0.0).astype(f32)
    has_r = jnp.where(me < blk - 1, 1.0, 0.0).astype(f32)
    has_rr = jnp.where(me < blk - 2, 1.0, 0.0).astype(f32)

    lift = lift_ref[...]
    pick = (lax.broadcasted_iota(jnp.int32, (8, 64), 1) % 8
            == lax.broadcasted_iota(jnp.int32, (8, 64), 0))
    tiled = dot(lift, jnp.where(pick, 1.0, 0.0).astype(bf16))
    col_month = lax.broadcasted_iota(jnp.int32, (64, 64), 1) // 8
    placed = [jnp.where(col_month == i, tiled, 0.0) for i in range(8)]
    placed_b = [x.astype(bf16) for x in placed]
    inner_rows = []
    for j in range(6):
        acc = dot(mk_ref[0, 0], placed_b[j])
        acc = acc + dot(mk_ref[0, 1], placed_b[j + 1])
        acc = acc + dot(mk_ref[0, 2], placed_b[j + 2])
        inner_rows.append(acc)
    both = rows(*inner_rows, *placed[1:7])
    both_hi = both.astype(bf16).astype(f32)
    both_lo = both - both_hi
    wf1[...] = lanes(both_hi, both_lo, both_hi, jnp.zeros_like(both)).astype(bf16)
    flipped_hi = jnp.transpose(both_hi)
    flipped_lo = jnp.transpose(both_lo)
    wb1[...] = rows(flipped_hi, flipped_lo).astype(bf16)

    def mk(k):
        return mk_ref[1, k].astype(f32)

    wf2[...] = lanes(mk(0) * has_l, mk(1), mk(2) * has_r).astype(bf16)
    wb2[...] = rows(
        jnp.transpose(mk(0)) * has_l, jnp.transpose(mk(1)), jnp.transpose(mk(2)) * has_r
    ).astype(bf16)
    wf3[...] = grid_weights(lambda a, b: gk_ref[0, a, b].astype(f32))
    wf4[...] = grid_weights(lambda a, b: gk_ref[1, a, b].astype(f32))
    wb3[...] = grid_weights(lambda a, b: jnp.transpose(gk_ref[0, 2 - a, 2 - b].astype(f32)))
    wb4[...] = grid_weights(lambda a, b: jnp.transpose(gk_ref[1, 2 - a, 2 - b].astype(f32)))
    read = read_ref[...].astype(f32)
    zero_read = jnp.zeros((8, 64), f32)
    wide = rows(lanes(read, zero_read), lanes(zero_read, read))
    wread[...] = wide.astype(bf16)
    tall = jnp.transpose(wide)
    wreadt[...] = lanes(tall, tall).astype(bf16)

    local = month_ref[...] - 2 * me
    owned = jnp.logical_and(local >= 0, local < 2)
    cell = cell_ref[...]
    row_of = jnp.where(owned, (local * 16 + lax.shift_right_logical(cell, 7)) * 8 + var_ref[...], -1)
    lon_of = jnp.bitwise_and(cell, 127)
    weight = pw_ref[...]
    weighted = weight * obs_ref[...]
    w_hi = weight.astype(bf16).astype(f32)
    w_lo = (weight - w_hi).astype(bf16).astype(f32)
    b_hi = weighted.astype(bf16).astype(f32)
    b_lo = (weighted - b_hi).astype(bf16).astype(f32)
    b_sum = b_hi + b_lo
    spread_terms = jnp.where(owned, b_sum * b_sum / (w_hi + w_lo), 0.0)
    within = (spread_terms[0:8] + spread_terms[8:16]) + (spread_terms[16:24] + spread_terms[24:32])
    row_iota = lax.broadcasted_iota(jnp.int32, (256, 128), 0)
    lon_iota = lax.broadcasted_iota(jnp.int32, (128, 128), 0)
    for c in range(4):
        lhs, rhs = [], []
        for r in range(8 * c, 8 * c + 8):
            lhs.append(jnp.where(row_iota == row_of[r:r + 1], 1.0, 0.0).astype(bf16))
            at = lon_iota == lon_of[r:r + 1]
            rhs.append(rows(*[
                jnp.where(at, x[r:r + 1], 0.0).astype(bf16) for x in (w_hi, w_lo, b_hi, b_lo)
            ]))
        part = dot_nt(lanes(*lhs), lanes(*rhs))
        if c == 0:
            field[...] = part
        else:
            field[...] += part
    w_field = field[:, 0:128] + field[:, 128:256]
    b_field = field[:, 256:384] + field[:, 384:512]
    mean = jnp.where(w_field > 0.0, b_field / jnp.where(w_field > 0.0, w_field, 1.0), 0.0)
    field[:, 0:128] = w_field
    field[:, 128:256] = mean
    taken = b_field * mean
    for r in range(32):
        within = within - taken[8 * r:8 * r + 8]

    zero_row = jnp.zeros((64, 256), bf16)
    for ref in (h2s, h3s, s4s, s3s):
        ref[0] = zero_row
        ref[17] = zero_row

    lane = lax.broadcasted_iota(jnp.int32, (128, 128), 1)
    first, last = lane == 0, lane == 127

    for copy in halo:
        copy.wait_recv()

    def month_step(q, carry):
        highs, lows = [], []
        for i in range(2):
            l = 2 * q + i
            prev = halo_l[l].astype(f32) * has_l
            nxt = halo_r[l].astype(f32) * has_r
            prev2 = halo_ll[q].astype(f32)[8 * i:8 * i + 8] * has_ll
            nxt2 = halo_rr[q].astype(f32)[8 * i:8 * i + 8] * has_rr
            own = rows(sample_ref[0, l], sample_ref[1, l])
            own_hi = own.astype(bf16).astype(f32)
            highs.append(rows(prev2, prev, own_hi, nxt, nxt2))
            z = jnp.zeros((24, 128), f32)
            lows.append(rows(z, own - own_hi, z))
        high = lanes(*highs)
        src = rows(high, high, lanes(*lows), jnp.zeros((64, 256), f32)).astype(bf16)
        out = dot(wf1[...], src)
        gel, der = gelu_parts(out[0:384])
        g1[q] = der
        hidden = out[384:768] + gel
        hidden_b = hidden.astype(bf16)
        for m in range(2):
            src2 = rows(*[hidden_b[64 * j:64 * j + 64] for j in (m, m + 2, m + 4)])
            gel2, der2 = gelu_parts(dot(wf2[...], src2))
            g2[q, m] = der2
            nxt_h = (hidden[64 * (m + 2):64 * (m + 3)] + gel2).astype(bf16)
            for i in range(2):
                h2s[2 * q + i + 1, :, 128 * m:128 * m + 128] = nxt_h[:, 128 * i:128 * i + 128]
        return carry

    lax.fori_loop(0, 8, month_step, 0)

    def window(ref, q):
        return ref[pl.ds(2 * q, 4)].reshape(256, 256)

    def pair(ref, q, at):
        return ref[pl.ds(2 * q + at, 2)].reshape(128, 256)

    def grid_step(q, carry):
        inner = lon_sum(dot(wf3[...], window(h2s, q)), first, last)
        gel, der = gelu_parts(inner)
        g3[q] = der
        h3s[pl.ds(2 * q + 1, 2)] = (pair(h2s, q, 1).astype(f32) + gel).astype(bf16).reshape(2, 64, 256)
        return carry

    lax.fori_loop(0, 8, grid_step, 0)

    def top_step(q, total):
        inner = lon_sum(dot(wf4[...], window(h3s, q)), first, last)
        gel, der = gelu_parts(inner)
        hidden = (pair(h3s, q, 1).astype(f32) + gel).astype(bf16)
        score = dot(wread[...], hidden)
        forces = []
        for i in range(2):
            l = 2 * q + i
            line = []
            for m in range(2):
                sc = score[8 * i:8 * i + 8, 128 * m:128 * m + 128]
                sm = sample_ref[m, l]
                at = pl.ds((m * 16 + l) * 8, 8)
                w = field[at, 0:128]
                delta = sm + tweedie_gain * sc - field[at, 128:256]
                pull = w * delta
                total = total + pull * delta
                force = guide_gain * pull
                base[m, l] = sm + step_size * sc + noise_gain * noise_ref[m, l]
                grad[m, l] = force
                line.append(tweedie_gain * force)
            forces.append(lanes(*line))
        force = rows(*forces)
        force_hi = force.astype(bf16).astype(f32)
        src = rows(force_hi, force - force_hi).astype(bf16)
        adj = dot(wreadt[...], src)
        a4[q] = adj
        s4s[pl.ds(2 * q + 1, 2)] = (adj * der).astype(bf16).reshape(2, 64, 256)
        return total

    total = lax.fori_loop(0, 8, top_step, within)

    psend[...] = total
    sums = [
        remote(psend, pbuf.at[k], ps_sem.at[k], pr_sem.at[k], k) for k in range(1, blk)
    ]
    for copy in sums:
        copy.start()

    def back_step(q, carry):
        adj = a4[q] + lon_sum(dot(wb4[...], window(s4s, q)), first, last)
        a3[q] = adj
        s3s[pl.ds(2 * q + 1, 2)] = (adj * g3[q]).astype(bf16).reshape(2, 64, 256)
        return carry

    lax.fori_loop(0, 8, back_step, 0)

    def low_step(q, carry):
        adj2 = a3[q] + lon_sum(dot(wb3[...], window(s3s, q)), first, last)
        own, pushed = [], []
        for m in range(2):
            cols = slice(128 * m, 128 * m + 128)
            adj = lanes(adj2[0:64, cols], adj2[64:128, cols])
            own.append(adj)
            scaled = (adj * g2[q, m]).astype(bf16)
            pushed.append(dot(wb2[...], scaled))
        adj1 = rows(
            pushed[0][0:64], pushed[1][0:64],
            own[0] + pushed[0][64:128], own[1] + pushed[1][64:128],
            pushed[0][128:192], pushed[1][128:192],
        )
        scaled1 = (adj1 * g1[q]).astype(bf16)
        both = dot(wb1[...], rows(scaled1, adj1.astype(bf16)))
        part = both[0:64] + both[64:128]
        for i in range(2):
            l = 2 * q + i
            cols = slice(128 * i, 128 * i + 128)
            gs_l[l] = part[8:24, cols].astype(bf16)
            gs_r[l] = part[40:56, cols].astype(bf16)
            for m in range(2):
                grad[m, l] += part[24 + 8 * m:32 + 8 * m, cols]
        gs_ll[q] = rows(part[0:8, 0:128], part[0:8, 128:256]).astype(bf16)
        gs_rr[q] = rows(part[56:64, 0:128], part[56:64, 128:256]).astype(bf16)
        return carry

    lax.fori_loop(0, 8, low_step, 0)
    back = [
        remote(gs_r, gr_l, gs_sem.at[0], gr_sem.at[0], 1),
        remote(gs_l, gr_r, gs_sem.at[1], gr_sem.at[1], -1),
        remote(gs_rr, gr_ll, gs_sem.at[2], gr_sem.at[2], 2),
        remote(gs_ll, gr_rr, gs_sem.at[3], gr_sem.at[3], -2),
    ]
    for copy in back:
        copy.start()

    for copy in sums:
        copy.wait_recv()
    tile = psend[...]
    for k in range(1, blk):
        tile = tile + pbuf[k]
    full = jnp.sum(jnp.sum(tile, axis=1, keepdims=True), axis=0, keepdims=True)
    norm = jnp.sqrt(full / 4096.0 + 1e-05)
    scale = jnp.broadcast_to(step_size / norm, (8, 128))

    for copy in back:
        copy.wait_recv()
    for q in range(8):
        far_l = gr_ll[q].astype(f32) * has_ll
        far_r = gr_rr[q].astype(f32) * has_rr
        for i in range(2):
            l = 2 * q + i
            near = gr_l[l].astype(f32) * has_l + gr_r[l].astype(f32) * has_r
            far = (far_l[8 * i:8 * i + 8], far_r[8 * i:8 * i + 8])
            for m in range(2):
                g = grad[m, l] + near[8 * m:8 * m + 8] + far[m]
                out_ref[m, l] = base[m, l] - scale * g

    for copy in halo + sums + back:
        copy.wait_send()


def shards(
    blk,
    sample, fresh_noise, proxy_month, proxy_cell, proxy_var, observed, proxy_weight,
    lift_weight, month_kernels, grid_kernels, read_weight,
):
    def grid(x):
        return x.reshape(32, 128)

    vmem = pltpu.VMEM
    dma = pltpu.SemaphoreType.DMA
    scratch = [
        vmem((16, 16, 128), bf16), vmem((8, 16, 128), bf16), vmem((8, 16, 128), bf16),
        vmem((16, 16, 128), bf16), vmem((16, 16, 128), bf16),
        vmem((8, 16, 128), bf16), vmem((8, 16, 128), bf16),
        vmem((768, 256), bf16), vmem((64, 192), bf16),
        vmem((384, 256), bf16), vmem((384, 256), bf16), vmem((384, 256), bf16), vmem((384, 256), bf16),
        vmem((192, 64), bf16), vmem((128, 768), bf16),
        vmem((16, 128), bf16), vmem((128, 32), bf16),
        vmem((256, 512), f32),
        vmem((8, 384, 256), f32), vmem((8, 2, 64, 256), f32),
        vmem((8, 128, 256), f32), vmem((8, 128, 256), f32),
        vmem((18, 64, 256), bf16), vmem((18, 64, 256), bf16),
        vmem((18, 64, 256), bf16), vmem((18, 64, 256), bf16),
        vmem((8, 128, 256), f32), vmem((8, 128, 256), f32),
        vmem((2, 16, 8, 128), f32), vmem((2, 16, 8, 128), f32),
        vmem((16, 16, 128), bf16), vmem((16, 16, 128), bf16),
        vmem((8, 16, 128), bf16), vmem((8, 16, 128), bf16),
        vmem((16, 16, 128), bf16), vmem((16, 16, 128), bf16),
        vmem((8, 16, 128), bf16), vmem((8, 16, 128), bf16),
        vmem((8, 128), f32), vmem((blk, 8, 128), f32),
        dma((4,)), dma((4,)), dma((4,)), dma((4,)), dma((blk,)), dma((blk,)),
    ]
    return pl.pallas_call(
        functools.partial(kernel, blk),
        out_shape=jax.ShapeDtypeStruct(sample.shape, f32),
        in_specs=[pl.BlockSpec(memory_space=pltpu.VMEM)] * 11,
        out_specs=pl.BlockSpec(memory_space=pltpu.VMEM),
        scratch_shapes=scratch,
        compiler_params=pltpu.CompilerParams(collective_id=0, has_side_effects=True),
        name="guided_step",
    )(
        sample, fresh_noise, grid(proxy_month), grid(proxy_cell), grid(proxy_var),
        grid(observed), grid(proxy_weight), lift_weight, month_kernels, grid_kernels, read_weight,
    )


def solution(mesh):
    in_specs = (
        P(("win", "blk"), None, None, None),
        P(("win", "blk"), None, None, None),
        P("win"),
        P("win"),
        P("win"),
        P("win"),
        P("win"),
        P(),
        P(),
        P(),
        P(),
    )
    out_specs = P(("win", "blk"), None, None, None)
    return jax.shard_map(
        functools.partial(shards, mesh.shape["blk"]),
        mesh=mesh, in_specs=in_specs, out_specs=out_specs, check_vma=False,
    )
```

```python
import functools

import jax
import jax.numpy as jnp
from jax import lax
from jax.experimental import pallas as pl
from jax.experimental.pallas import tpu as pltpu
from jax.sharding import PartitionSpec as P

tweedie_gain = 0.5
step_size = 0.25
guide_gain = 4.0
noise_gain = 0.5**0.5

f32 = jnp.float32
bf16 = jnp.bfloat16
MESH = pl.DeviceIdType.MESH

gelu_c = 0.7978845608028654
gelu_ca = gelu_c * 0.044715


def gelu_parts(x):
    x2 = x * x
    u = x * (gelu_c + gelu_ca * x2)
    h = 0.5 * jnp.tanh(u) + 0.5
    g = x * h
    dg = h + (g - g * h) * (2.0 * gelu_c + 6.0 * gelu_ca * x2)
    return g, dg


def dot(a, b):
    return jnp.dot(a, b, preferred_element_type=f32)


def dot_nt(a, b):
    return lax.dot_general(a, b, (((1,), (1,)), ((), ())), preferred_element_type=f32)


def lanes(*parts):
    return jnp.concatenate(parts, axis=1)


def rows(*parts):
    return jnp.concatenate(parts, axis=0)


def lon_sum(out, first, last):
    halves = []
    for m in range(2):
        cols = slice(128 * m, 128 * (m + 1))
        left = pltpu.roll(out[0:128, cols], 1, 1)
        right = pltpu.roll(out[256:384, cols], 127, 1)
        total = out[128:256, cols] + jnp.where(first, 0.0, left) + jnp.where(last, 0.0, right)
        halves.append(total)
    return lanes(*halves)


def grid_weights(block):
    zero = jnp.zeros((64, 64), f32)
    out = []
    for b in range(3):
        k0, k1, k2 = block(0, b), block(1, b), block(2, b)
        out.append(lanes(k0, k1, k2, zero))
        out.append(lanes(zero, k0, k1, k2))
    return rows(*out).astype(bf16)


def kernel(
    blk,
    sample_in, noise_in, month_in, cell_in, var_in, obs_in, pw_in,
    lift_in, mk_in, gk_in, read_in,
    out_ref,
    sample_ref, noise_ref, month_ref, cell_ref, var_ref, obs_ref, pw_ref,
    lift_ref, mk_ref, gk_ref, read_ref,
    send_pair, send_lo, send_hi, halo_l, halo_r, halo_ll, halo_rr,
    wf1, wf2, wf3, wf4, wb4, wb3, wb2, wb1, wread, wreadt,
    field,
    g1, g2, g3, g4, h2s, h3s, s4s, s3s, a4, a3,
    base, grad,
    gs_l, gs_r, gs_ll, gs_rr, gr_l, gr_r, gr_ll, gr_rr,
    psend, pbuf,
    hs_sem, hr_sem, gs_sem, gr_sem, ps_sem, pr_sem, in_sem, near_sem, far_sem,
):
    me = lax.axis_index("blk")

    def peer(k):
        return lax.rem(me + k + blk, blk)

    def remote(src, dst, ssem, rsem, k):
        return pltpu.make_async_remote_copy(
            src_ref=src, dst_ref=dst, send_sem=ssem, recv_sem=rsem,
            device_id={"blk": peer(k)}, device_id_type=MESH,
        )

    def signal(sem, k):
        pl.semaphore_signal(sem, inc=1, device_id={"blk": peer(k)}, device_id_type=MESH)

    barrier = pltpu.get_barrier_semaphore()
    for k in (2, -2, 1, -1):
        signal(barrier, k)

    loads = [
        pltpu.make_async_copy(src, dst, in_sem.at[n])
        for n, (src, dst) in enumerate((
            (sample_in, sample_ref), (mk_in, mk_ref), (lift_in, lift_ref), (gk_in, gk_ref),
            (read_in, read_ref), (month_in, month_ref), (cell_in, cell_ref), (var_in, var_ref),
            (obs_in, obs_ref), (pw_in, pw_ref), (noise_in, noise_ref),
        ))
    ]
    for copy in loads:
        copy.start()
    loads[0].wait()

    for l in range(16):
        send_pair[l] = rows(sample_ref[0, l], sample_ref[1, l]).astype(bf16)
    for q in range(8):
        send_lo[q] = rows(sample_ref[0, 2 * q], sample_ref[0, 2 * q + 1]).astype(bf16)
        send_hi[q] = rows(sample_ref[1, 2 * q], sample_ref[1, 2 * q + 1]).astype(bf16)

    pl.semaphore_wait(barrier, 4)

    def halo_part(n, k, src, dst, part, size):
        at = pl.ds(part * size, size)
        return remote(src.at[at], dst.at[at], hs_sem.at[n, part], hr_sem.at[n, part], k)

    halo = [
        [
            halo_part(2, 2, send_hi, halo_ll, part, 4),
            halo_part(3, -2, send_lo, halo_rr, part, 4),
            halo_part(0, 1, send_pair, halo_l, part, 8),
            halo_part(1, -1, send_pair, halo_r, part, 8),
        ]
        for part in range(2)
    ]
    for part in halo:
        for copy in part:
            copy.start()
    for k in (2, -2):
        signal(near_sem, k)
    for copy in loads[1:10]:
        copy.wait()

    has_l = jnp.where(me > 0, 1.0, 0.0).astype(f32)
    has_ll = jnp.where(me > 1, 1.0, 0.0).astype(f32)
    has_r = jnp.where(me < blk - 1, 1.0, 0.0).astype(f32)
    has_rr = jnp.where(me < blk - 2, 1.0, 0.0).astype(f32)

    lift = lift_ref[...]
    pick = (lax.broadcasted_iota(jnp.int32, (8, 64), 1) % 8
            == lax.broadcasted_iota(jnp.int32, (8, 64), 0))
    pick = jnp.where(pick, 1.0, 0.0).astype(bf16)
    tiled = lax.dot_general(
        lift, pick, (((0,), (0,)), ((), ())), preferred_element_type=f32
    )
    col_month = lax.broadcasted_iota(jnp.int32, (64, 64), 1) // 8
    placed = [jnp.where(col_month == i, tiled, 0.0) for i in range(8)]
    placed_b = [x.astype(bf16) for x in placed]
    inner_rows = []
    for j in range(6):
        acc = dot(mk_ref[0, 0], placed_b[j])
        acc = acc + dot(mk_ref[0, 1], placed_b[j + 1])
        acc = acc + dot(mk_ref[0, 2], placed_b[j + 2])
        inner_rows.append(acc)
    both = rows(*inner_rows, *placed[1:7])
    both_hi = both.astype(bf16).astype(f32)
    both_lo = both - both_hi
    wf1[...] = lanes(both_hi, both_lo, both_hi, jnp.zeros_like(both)).astype(bf16)
    flipped_hi = jnp.transpose(both_hi)
    flipped_lo = jnp.transpose(both_lo)
    wb1[...] = rows(flipped_hi, flipped_lo).astype(bf16)

    def mk(k):
        return mk_ref[1, k].astype(f32)

    wf2[...] = lanes(mk(0) * has_l, mk(1), mk(2) * has_r).astype(bf16)
    wb2[...] = rows(
        jnp.transpose(mk(0)) * has_l, jnp.transpose(mk(1)), jnp.transpose(mk(2)) * has_r
    ).astype(bf16)
    wf3[...] = grid_weights(lambda a, b: gk_ref[0, a, b].astype(f32))
    wf4[...] = grid_weights(lambda a, b: gk_ref[1, a, b].astype(f32))
    wb3[...] = grid_weights(lambda a, b: jnp.transpose(gk_ref[0, 2 - a, 2 - b].astype(f32)))
    wb4[...] = grid_weights(lambda a, b: jnp.transpose(gk_ref[1, 2 - a, 2 - b].astype(f32)))
    read = read_ref[...].astype(f32)
    zero_read = jnp.zeros((8, 64), f32)
    wide = rows(lanes(read, zero_read), lanes(zero_read, read))
    wread[...] = wide.astype(bf16)
    tall = jnp.transpose(wide)
    wreadt[...] = lanes(tall, tall).astype(bf16)

    local = month_ref[...] - 2 * me
    owned = jnp.logical_and(local >= 0, local < 2)
    cell = cell_ref[...]
    row_of = jnp.where(owned, (local * 16 + lax.shift_right_logical(cell, 7)) * 8 + var_ref[...], -1)
    lon_of = jnp.bitwise_and(cell, 127)
    weight = pw_ref[...]
    weighted = weight * obs_ref[...]
    w_hi = weight.astype(bf16).astype(f32)
    w_lo = (weight - w_hi).astype(bf16).astype(f32)
    b_hi = weighted.astype(bf16).astype(f32)
    b_lo = (weighted - b_hi).astype(bf16).astype(f32)
    b_sum = b_hi + b_lo
    spread_terms = jnp.where(owned, b_sum * b_sum / (w_hi + w_lo), 0.0)
    within = (spread_terms[0:8] + spread_terms[8:16]) + (spread_terms[16:24] + spread_terms[24:32])
    row_iota = lax.broadcasted_iota(jnp.int32, (256, 128), 0)
    lon_iota = lax.broadcasted_iota(jnp.int32, (128, 128), 0)
    for c in range(4):
        lhs, rhs = [], []
        for r in range(8 * c, 8 * c + 8):
            lhs.append(jnp.where(row_iota == row_of[r:r + 1], 1.0, 0.0).astype(bf16))
            at = lon_iota == lon_of[r:r + 1]
            rhs.append(rows(*[
                jnp.where(at, x[r:r + 1], 0.0).astype(bf16) for x in (w_hi, w_lo, b_hi, b_lo)
            ]))
        part = dot_nt(lanes(*lhs), lanes(*rhs))
        if c == 0:
            field[...] = part
        else:
            field[...] += part
    w_field = field[:, 0:128] + field[:, 128:256]
    b_field = field[:, 256:384] + field[:, 384:512]
    mean = jnp.where(w_field > 0.0, b_field / jnp.where(w_field > 0.0, w_field, 1.0), 0.0)
    field[:, 0:128] = w_field
    field[:, 128:256] = mean
    taken = b_field * mean
    for r in range(32):
        within = within - taken[8 * r:8 * r + 8]

    zero_row = jnp.zeros((64, 256), bf16)
    for ref in (h2s, h3s, s4s, s3s):
        ref[0] = zero_row
        ref[17] = zero_row

    lane = lax.broadcasted_iota(jnp.int32, (128, 128), 1)
    first, last = lane == 0, lane == 127

    def month_step(q, carry):
        highs, lows = [], []
        for i in range(2):
            l = 2 * q + i
            prev = halo_l[l].astype(f32) * has_l
            nxt = halo_r[l].astype(f32) * has_r
            prev2 = halo_ll[q].astype(f32)[8 * i:8 * i + 8] * has_ll
            nxt2 = halo_rr[q].astype(f32)[8 * i:8 * i + 8] * has_rr
            own = rows(sample_ref[0, l], sample_ref[1, l])
            own_hi = own.astype(bf16).astype(f32)
            highs.append(rows(prev2, prev, own_hi, nxt, nxt2))
            z = jnp.zeros((24, 128), f32)
            lows.append(rows(z, own - own_hi, z))
        high = lanes(*highs)
        src = rows(high, high, lanes(*lows), jnp.zeros((64, 256), f32)).astype(bf16)
        out = dot(wf1[...], src)
        gel, der = gelu_parts(out[0:384])
        g1[q] = der
        hidden = out[384:768] + gel
        hidden_b = hidden.astype(bf16)
        for m in range(2):
            src2 = rows(*[hidden_b[64 * j:64 * j + 64] for j in (m, m + 2, m + 4)])
            gel2, der2 = gelu_parts(dot(wf2[...], src2))
            g2[q, m] = der2
            nxt_h = (hidden[64 * (m + 2):64 * (m + 3)] + gel2).astype(bf16)
            for i in range(2):
                h2s[2 * q + i + 1, :, 128 * m:128 * m + 128] = nxt_h[:, 128 * i:128 * i + 128]
        return carry

    pl.semaphore_wait(near_sem, 2)
    for k in (4, -4):
        signal(far_sem, k)
    for part in range(2):
        for copy in halo[part]:
            copy.wait_recv()
        lax.fori_loop(4 * part, 4 * part + 4, month_step, 0, unroll=4)
    loads[10].wait()

    def window(ref, q):
        return ref[pl.ds(2 * q, 4)].reshape(256, 256)

    def pair(ref, q, at):
        return ref[pl.ds(2 * q + at, 2)].reshape(128, 256)

    def grid_step(q, carry):
        inner = lon_sum(dot(wf3[...], window(h2s, q)), first, last)
        gel, der = gelu_parts(inner)
        g3[q] = der
        h3s[pl.ds(2 * q + 1, 2)] = (pair(h2s, q, 1).astype(f32) + gel).astype(bf16).reshape(2, 64, 256)
        return carry

    lax.fori_loop(0, 8, grid_step, 0, unroll=8)

    def top_step(q, total):
        inner = lon_sum(dot(wf4[...], window(h3s, q)), first, last)
        gel, der = gelu_parts(inner)
        hidden = (pair(h3s, q, 1).astype(f32) + gel).astype(bf16)
        score = dot(wread[...], hidden)
        forces = []
        for i in range(2):
            l = 2 * q + i
            line = []
            for m in range(2):
                sc = score[8 * i:8 * i + 8, 128 * m:128 * m + 128]
                sm = sample_ref[m, l]
                at = pl.ds((m * 16 + l) * 8, 8)
                w = field[at, 0:128]
                delta = sm + tweedie_gain * sc - field[at, 128:256]
                pull = w * delta
                total = total + pull * delta
                force = guide_gain * pull
                base[m, l] = sm + step_size * sc + noise_gain * noise_ref[m, l]
                grad[m, l] = force
                line.append(tweedie_gain * force)
            forces.append(lanes(*line))
        force = rows(*forces)
        force_hi = force.astype(bf16).astype(f32)
        src = rows(force_hi, force - force_hi).astype(bf16)
        adj = dot(wreadt[...], src)
        a4[q] = adj
        s4s[pl.ds(2 * q + 1, 2)] = (adj * der).astype(bf16).reshape(2, 64, 256)
        return total

    total = lax.fori_loop(0, 8, top_step, within, unroll=8)

    psend[...] = total
    pl.semaphore_wait(far_sem, 2)
    sums = [
        remote(psend, pbuf.at[k], ps_sem.at[k], pr_sem.at[k], k) for k in range(1, blk)
    ]
    for copy in sums:
        copy.start()

    def back_step(q, carry):
        adj = a4[q] + lon_sum(dot(wb4[...], window(s4s, q)), first, last)
        a3[q] = adj
        s3s[pl.ds(2 * q + 1, 2)] = (adj * g3[q]).astype(bf16).reshape(2, 64, 256)
        return carry

    lax.fori_loop(0, 8, back_step, 0, unroll=8)

    def low_step(q, carry):
        adj2 = a3[q] + lon_sum(dot(wb3[...], window(s3s, q)), first, last)
        own, pushed = [], []
        for m in range(2):
            cols = slice(128 * m, 128 * m + 128)
            adj = lanes(adj2[0:64, cols], adj2[64:128, cols])
            own.append(adj)
            scaled = (adj * g2[q, m]).astype(bf16)
            pushed.append(dot(wb2[...], scaled))
        adj1 = rows(
            pushed[0][0:64], pushed[1][0:64],
            own[0] + pushed[0][64:128], own[1] + pushed[1][64:128],
            pushed[0][128:192], pushed[1][128:192],
        )
        scaled1 = (adj1 * g1[q]).astype(bf16)
        both = dot(wb1[...], rows(scaled1, adj1.astype(bf16)))
        part = both[0:64] + both[64:128]
        for i in range(2):
            l = 2 * q + i
            cols = slice(128 * i, 128 * i + 128)
            gs_l[l] = part[8:24, cols].astype(bf16)
            gs_r[l] = part[40:56, cols].astype(bf16)
            for m in range(2):
                grad[m, l] += part[24 + 8 * m:32 + 8 * m, cols]
        gs_ll[q] = rows(part[0:8, 0:128], part[0:8, 128:256]).astype(bf16)
        gs_rr[q] = rows(part[56:64, 0:128], part[56:64, 128:256]).astype(bf16)
        return carry

    def back_part(n, k, src, dst, part, size):
        at = pl.ds(part * size, size)
        return remote(src.at[at], dst.at[at], gs_sem.at[n, part], gr_sem.at[n, part], k)

    back = [
        [
            back_part(2, 2, gs_rr, gr_ll, part, 2),
            back_part(3, -2, gs_ll, gr_rr, part, 2),
            back_part(0, 1, gs_r, gr_l, part, 4),
            back_part(1, -1, gs_l, gr_r, part, 4),
        ]
        for part in range(4)
    ]
    for part in range(4):
        lax.fori_loop(2 * part, 2 * part + 2, low_step, 0, unroll=2)
        for copy in back[part]:
            copy.start()

    for copy in sums:
        copy.wait_recv()
    tile = psend[...]
    for k in range(1, blk):
        tile = tile + pbuf[k]
    full = jnp.sum(jnp.sum(tile, axis=1, keepdims=True), axis=0, keepdims=True)
    norm = jnp.sqrt(full / month_ref.size + 1e-05)
    scale = jnp.broadcast_to(step_size / norm, (8, 128))

    for q in range(8):
        if q % 2 == 0:
            for copy in back[q // 2]:
                copy.wait_recv()
        far_l = gr_ll[q].astype(f32) * has_ll
        far_r = gr_rr[q].astype(f32) * has_rr
        for i in range(2):
            l = 2 * q + i
            near = gr_l[l].astype(f32) * has_l + gr_r[l].astype(f32) * has_r
            far = (far_l[8 * i:8 * i + 8], far_r[8 * i:8 * i + 8])
            for m in range(2):
                g = grad[m, l] + near[8 * m:8 * m + 8] + far[m]
                out_ref[m, l] = base[m, l] - scale * g

    for copy in sum(halo + back, sums):
        copy.wait_send()


def shards(
    blk,
    sample, fresh_noise, proxy_month, proxy_cell, proxy_var, observed, proxy_weight,
    lift_weight, month_kernels, grid_kernels, read_weight,
):
    def grid(x):
        return x.reshape(32, 128)

    vmem = pltpu.VMEM
    dma = pltpu.SemaphoreType.DMA
    scratch = [
        vmem(sample.shape, f32), vmem(sample.shape, f32),
        vmem((32, 128), jnp.int32), vmem((32, 128), jnp.int32), vmem((32, 128), jnp.int32),
        vmem((32, 128), f32), vmem((32, 128), f32),
        vmem((8, 64), bf16), vmem(month_kernels.shape, bf16), vmem(grid_kernels.shape, bf16),
        vmem((8, 64), bf16),
        vmem((16, 16, 128), bf16), vmem((8, 16, 128), bf16), vmem((8, 16, 128), bf16),
        vmem((16, 16, 128), bf16), vmem((16, 16, 128), bf16),
        vmem((8, 16, 128), bf16), vmem((8, 16, 128), bf16),
        vmem((768, 256), bf16), vmem((64, 192), bf16),
        vmem((384, 256), bf16), vmem((384, 256), bf16), vmem((384, 256), bf16), vmem((384, 256), bf16),
        vmem((192, 64), bf16), vmem((128, 768), bf16),
        vmem((16, 128), bf16), vmem((128, 32), bf16),
        vmem((256, 512), f32),
        vmem((8, 384, 256), f32), vmem((8, 2, 64, 256), f32),
        vmem((8, 128, 256), f32), vmem((8, 128, 256), f32),
        vmem((18, 64, 256), bf16), vmem((18, 64, 256), bf16),
        vmem((18, 64, 256), bf16), vmem((18, 64, 256), bf16),
        vmem((8, 128, 256), f32), vmem((8, 128, 256), f32),
        vmem((2, 16, 8, 128), f32), vmem((2, 16, 8, 128), f32),
        vmem((16, 16, 128), bf16), vmem((16, 16, 128), bf16),
        vmem((8, 16, 128), bf16), vmem((8, 16, 128), bf16),
        vmem((16, 16, 128), bf16), vmem((16, 16, 128), bf16),
        vmem((8, 16, 128), bf16), vmem((8, 16, 128), bf16),
        vmem((8, 128), f32), vmem((blk, 8, 128), f32),
        dma((4, 2)), dma((4, 2)), dma((4, 4)), dma((4, 4)), dma((blk,)), dma((blk,)), dma((11,)),
        pltpu.SemaphoreType.REGULAR, pltpu.SemaphoreType.REGULAR,
    ]
    return pl.pallas_call(
        functools.partial(kernel, blk),
        out_shape=jax.ShapeDtypeStruct(sample.shape, f32),
        in_specs=[pl.BlockSpec(memory_space=pl.ANY)] * 11,
        out_specs=pl.BlockSpec(memory_space=pltpu.VMEM),
        scratch_shapes=scratch,
        compiler_params=pltpu.CompilerParams(collective_id=0, has_side_effects=True),
        name="guided_step",
    )(
        sample, fresh_noise, grid(proxy_month), grid(proxy_cell), grid(proxy_var),
        grid(observed), grid(proxy_weight), lift_weight.T, month_kernels, grid_kernels, read_weight,
    )


def solution(mesh):
    in_specs = (
        P(("win", "blk"), None, None, None),
        P(("win", "blk"), None, None, None),
        P("win"),
        P("win"),
        P("win"),
        P("win"),
        P("win"),
        P(),
        P(),
        P(),
        P(),
    )
    out_specs = P(("win", "blk"), None, None, None)
    return jax.shard_map(
        functools.partial(shards, mesh.shape["blk"]),
        mesh=mesh, in_specs=in_specs, out_specs=out_specs, check_vma=False,
    )
```

```python
import functools

import jax
import jax.numpy as jnp
from jax import lax
from jax.experimental import pallas as pl
from jax.experimental.pallas import tpu as pltpu
from jax.sharding import PartitionSpec as P

tweedie_gain = 0.5
step_size = 0.25
guide_gain = 4.0
noise_gain = 0.5**0.5

f32 = jnp.float32
bf16 = jnp.bfloat16
MESH = pl.DeviceIdType.MESH

gelu_c = 0.7978845608028654
gelu_ca = gelu_c * 0.044715


def gelu_parts(x):
    x2 = x * x
    u = x * (gelu_c + gelu_ca * x2)
    h = 0.5 * jnp.tanh(u) + 0.5
    g = x * h
    dg = h + (g - g * h) * (2.0 * gelu_c + 6.0 * gelu_ca * x2)
    return g, dg


def dot(a, b):
    return jnp.dot(a, b, preferred_element_type=f32)


def dot_nt(a, b):
    return lax.dot_general(a, b, (((1,), (1,)), ((), ())), preferred_element_type=f32)


def lanes(*parts):
    return jnp.concatenate(parts, axis=1)


def rows(*parts):
    return jnp.concatenate(parts, axis=0)


def grid_weights(block):
    zero = jnp.zeros((64, 64), f32)
    upper, lower = [], []
    for b in range(3):
        taps = [block(a, b) for a in range(3)]
        upper += taps + [zero]
        lower += [zero] + taps
    return rows(lanes(*upper), lanes(*lower)).astype(bf16)


def kernel(
    blk,
    sample_in, noise_in, month_in, cell_in, var_in, obs_in, pw_in,
    lift_in, mk_in, gk_in, read_in,
    out_ref,
    sample_ref, noise_ref, month_ref, cell_ref, var_ref, obs_ref, pw_ref,
    lift_ref, mk_ref, gk_ref, read_ref,
    send_pair, send_lo, send_hi, halo_l, halo_r, halo_ll, halo_rr,
    wf1, wf2, wf3, wf4, wb4, wb3, wb2, wb1, wread, wreadt,
    field,
    h1s, h4s, a1s, g1, g2, g3, g4, h2s, h3s, s4s, s3s, a4, a3,
    base, grad,
    gs_l, gs_r, gs_ll, gs_rr, gr_l, gr_r, gr_ll, gr_rr,
    psend, pbuf,
    hs_sem, hr_sem, gs_sem, gr_sem, ps_sem, pr_sem, in_sem, near_sem, far_sem,
):
    me = lax.axis_index("blk")

    def peer(k):
        return lax.rem(me + k + blk, blk)

    def remote(src, dst, ssem, rsem, k):
        return pltpu.make_async_remote_copy(
            src_ref=src, dst_ref=dst, send_sem=ssem, recv_sem=rsem,
            device_id={"blk": peer(k)}, device_id_type=MESH,
        )

    def signal(sem, k):
        pl.semaphore_signal(sem, inc=1, device_id={"blk": peer(k)}, device_id_type=MESH)

    barrier = pltpu.get_barrier_semaphore()
    for k in (2, -2, 1, -1):
        signal(barrier, k)

    loads = [
        pltpu.make_async_copy(src, dst, in_sem.at[n])
        for n, (src, dst) in enumerate((
            (sample_in, sample_ref), (mk_in, mk_ref), (lift_in, lift_ref), (gk_in, gk_ref),
            (read_in, read_ref), (month_in, month_ref), (cell_in, cell_ref), (var_in, var_ref),
            (obs_in, obs_ref), (pw_in, pw_ref), (noise_in, noise_ref),
        ))
    ]
    for copy in loads:
        copy.start()
    loads[0].wait()

    for l in range(16):
        send_pair[l] = rows(sample_ref[0, l], sample_ref[1, l]).astype(bf16)
    for q in range(8):
        send_lo[q] = rows(sample_ref[0, 2 * q], sample_ref[0, 2 * q + 1]).astype(bf16)
        send_hi[q] = rows(sample_ref[1, 2 * q], sample_ref[1, 2 * q + 1]).astype(bf16)

    pl.semaphore_wait(barrier, 4)

    def halo_part(n, k, src, dst, part, size):
        at = pl.ds(part * size, size)
        return remote(src.at[at], dst.at[at], hs_sem.at[n, part], hr_sem.at[n, part], k)

    halo = [
        [
            halo_part(2, 2, send_hi, halo_ll, part, 2),
            halo_part(3, -2, send_lo, halo_rr, part, 2),
            halo_part(0, 1, send_pair, halo_l, part, 4),
            halo_part(1, -1, send_pair, halo_r, part, 4),
        ]
        for part in range(4)
    ]
    for part in halo:
        for copy in part:
            copy.start()
    for k in (2, -2):
        signal(near_sem, k)
    for copy in loads[1:10]:
        copy.wait()

    has_l = jnp.where(me > 0, 1.0, 0.0).astype(f32)
    has_ll = jnp.where(me > 1, 1.0, 0.0).astype(f32)
    has_r = jnp.where(me < blk - 1, 1.0, 0.0).astype(f32)
    has_rr = jnp.where(me < blk - 2, 1.0, 0.0).astype(f32)

    lift = lift_ref[...]
    pick = (lax.broadcasted_iota(jnp.int32, (8, 64), 1) % 8
            == lax.broadcasted_iota(jnp.int32, (8, 64), 0))
    pick = jnp.where(pick, 1.0, 0.0).astype(bf16)
    tiled = lax.dot_general(
        lift, pick, (((0,), (0,)), ((), ())), preferred_element_type=f32
    )
    col_month = lax.broadcasted_iota(jnp.int32, (64, 64), 1) // 8
    placed = [jnp.where(col_month == i, tiled, 0.0) for i in range(8)]
    placed_b = [x.astype(bf16) for x in placed]
    inner_rows = []
    for j in range(6):
        acc = dot(mk_ref[0, 0], placed_b[j])
        acc = acc + dot(mk_ref[0, 1], placed_b[j + 1])
        acc = acc + dot(mk_ref[0, 2], placed_b[j + 2])
        inner_rows.append(acc)
    both = rows(*[x for j in range(6) for x in (inner_rows[j], placed[j + 1])])
    both_hi = both.astype(bf16).astype(f32)
    both_lo = both - both_hi
    wf1[...] = lanes(both_hi, both_lo, both_hi, jnp.zeros_like(both)).astype(bf16)
    flipped_hi = jnp.transpose(both_hi)
    flipped_lo = jnp.transpose(both_lo)
    wb1[...] = rows(flipped_hi, flipped_lo).astype(bf16)

    def mk(k):
        return mk_ref[1, k].astype(f32)

    wf2[...] = lanes(mk(0) * has_l, mk(1), mk(2) * has_r).astype(bf16)
    wb2[...] = rows(
        jnp.transpose(mk(0)) * has_l, jnp.transpose(mk(1)), jnp.transpose(mk(2)) * has_r
    ).astype(bf16)
    wf3[...] = grid_weights(lambda a, b: gk_ref[0, a, b].astype(f32))
    wf4[...] = grid_weights(lambda a, b: gk_ref[1, a, b].astype(f32))
    wb3[...] = grid_weights(lambda a, b: jnp.transpose(gk_ref[0, 2 - a, 2 - b].astype(f32)))
    wb4[...] = grid_weights(lambda a, b: jnp.transpose(gk_ref[1, 2 - a, 2 - b].astype(f32)))
    read = read_ref[...].astype(f32)
    zero_read = jnp.zeros((8, 64), f32)
    wide = rows(lanes(read, zero_read), lanes(zero_read, read))
    wread[...] = wide.astype(bf16)
    tall = jnp.transpose(wide)
    wreadt[...] = lanes(tall, tall).astype(bf16)

    local = month_ref[...] - 2 * me
    owned = jnp.logical_and(local >= 0, local < 2)
    cell = cell_ref[...]
    row_of = jnp.where(owned, (local * 16 + lax.shift_right_logical(cell, 7)) * 8 + var_ref[...], -1)
    lon_of = jnp.bitwise_and(cell, 127)
    weight = pw_ref[...]
    weighted = weight * obs_ref[...]
    w_hi = weight.astype(bf16).astype(f32)
    w_lo = (weight - w_hi).astype(bf16).astype(f32)
    b_hi = weighted.astype(bf16).astype(f32)
    b_lo = (weighted - b_hi).astype(bf16).astype(f32)
    b_sum = b_hi + b_lo
    spread_terms = jnp.where(owned, b_sum * b_sum / (w_hi + w_lo), 0.0)
    within = (spread_terms[0:8] + spread_terms[8:16]) + (spread_terms[16:24] + spread_terms[24:32])
    row_iota = lax.broadcasted_iota(jnp.int32, (256, 128), 0)
    lon_iota = lax.broadcasted_iota(jnp.int32, (128, 128), 0)
    for c in range(4):
        lhs, rhs = [], []
        for r in range(8 * c, 8 * c + 8):
            lhs.append(jnp.where(row_iota == row_of[r:r + 1], 1.0, 0.0).astype(bf16))
            at = lon_iota == lon_of[r:r + 1]
            rhs.append(rows(*[
                jnp.where(at, x[r:r + 1], 0.0).astype(bf16) for x in (w_hi, w_lo, b_hi, b_lo)
            ]))
        part = dot_nt(lanes(*lhs), lanes(*rhs))
        if c == 0:
            field[...] = part
        else:
            field[...] += part
    w_field = field[:, 0:128] + field[:, 128:256]
    b_field = field[:, 256:384] + field[:, 384:512]
    mean = jnp.where(w_field > 0.0, b_field / jnp.where(w_field > 0.0, w_field, 1.0), 0.0)
    field[:, 0:128] = w_field
    field[:, 128:256] = mean
    taken = b_field * mean
    for r in range(32):
        within = within - taken[8 * r:8 * r + 8]

    zero_row = jnp.zeros((64, 256), bf16)
    for ref in (h2s, h3s, s4s, s3s):
        for tap in range(3):
            ref[tap, 0] = zero_row
            ref[tap, 17] = zero_row

    lane = lax.broadcasted_iota(jnp.int32, (128, 128), 1)
    first, last = lane == 0, lane == 127
    zero_half = jnp.zeros((128, 128), bf16)

    def window(ref, q):
        return rows(*[ref[tap, pl.ds(2 * q, 4)].reshape(256, 256) for tap in range(3)])

    def pair(ref, q):
        return ref[1, pl.ds(2 * q + 1, 2)].reshape(128, 256)

    def put(ref, q, value):
        left, right = [], []
        for m in range(2):
            half = value[:, 128 * m:128 * m + 128]
            left.append(jnp.where(first, zero_half, pltpu.roll(half, 1, 1)))
            right.append(jnp.where(last, zero_half, pltpu.roll(half, 127, 1)))
        at = pl.ds(2 * q + 1, 2)
        ref[0, at] = lanes(*left).reshape(2, 64, 256)
        ref[1, at] = value.reshape(2, 64, 256)
        ref[2, at] = lanes(*right).reshape(2, 64, 256)

    def month_step(q, carry):
        highs, lows = [], []
        for i in range(2):
            l = 2 * q + i
            prev = halo_l[l].astype(f32) * has_l
            nxt = halo_r[l].astype(f32) * has_r
            prev2 = halo_ll[q].astype(f32)[8 * i:8 * i + 8] * has_ll
            nxt2 = halo_rr[q].astype(f32)[8 * i:8 * i + 8] * has_rr
            own = rows(sample_ref[0, l], sample_ref[1, l])
            own_hi = own.astype(bf16).astype(f32)
            highs.append(rows(prev2, prev, own_hi, nxt, nxt2))
            z = jnp.zeros((24, 128), f32)
            lows.append(rows(z, own - own_hi, z))
        high = lanes(*highs)
        src = rows(high, high, lanes(*lows), jnp.zeros((64, 256), f32)).astype(bf16)
        out = dot(wf1[...], src).astype(bf16)
        hidden = []
        for j in range(6):
            gel, der = gelu_parts(out[128 * j:128 * j + 64])
            g1[q, 64 * j:64 * j + 64] = der
            hidden.append(out[128 * j + 64:128 * j + 128] + gel)
        h1s[q] = rows(*hidden)
        return carry

    def month_step2(q, carry):
        halves = []
        for m in range(2):
            src2 = rows(*[h1s[q, 64 * j:64 * j + 64] for j in (m, m + 2, m + 4)])
            gel2, der2 = gelu_parts(dot(wf2[...], src2).astype(bf16))
            g2[q, m] = der2
            nxt_h = h1s[q, 64 * (m + 2):64 * (m + 3)] + gel2
            halves.append(rows(nxt_h[:, 0:128], nxt_h[:, 128:256]))
        put(h2s, q, lanes(*halves))
        return carry

    pl.semaphore_wait(near_sem, 2)
    for k in (4, -4):
        signal(far_sem, k)
    for part in range(4):
        for copy in halo[part]:
            copy.wait_recv()
        lax.fori_loop(2 * part, 2 * part + 2, month_step, 0, unroll=2)
    lax.fori_loop(0, 8, month_step2, 0, unroll=8)
    loads[10].wait()

    def grid_step(q, carry):
        inner = dot(wf3[...], window(h2s, q))
        gel, der = gelu_parts(inner)
        g3[q] = der.astype(bf16)
        put(h3s, q, (pair(h2s, q).astype(f32) + gel).astype(bf16))
        return carry

    lax.fori_loop(0, 8, grid_step, 0, unroll=8)

    def last_step(q, carry):
        inner = dot(wf4[...], window(h3s, q))
        gel, der = gelu_parts(inner)
        g4[q] = der.astype(bf16)
        h4s[q] = (pair(h3s, q).astype(f32) + gel).astype(bf16)
        return carry

    lax.fori_loop(0, 8, last_step, 0, unroll=8)

    def top_step(q, total):
        score = dot(wread[...], h4s[q])
        forces = []
        for i in range(2):
            l = 2 * q + i
            line = []
            for m in range(2):
                sc = score[8 * i:8 * i + 8, 128 * m:128 * m + 128]
                sm = sample_ref[m, l]
                at = pl.ds((m * 16 + l) * 8, 8)
                w = field[at, 0:128]
                delta = sm + tweedie_gain * sc - field[at, 128:256]
                pull = w * delta
                total = total + pull * delta
                force = guide_gain * pull
                base[m, l] = sm + step_size * sc + noise_gain * noise_ref[m, l]
                grad[m, l] = force
                line.append(tweedie_gain * force)
            forces.append(lanes(*line))
        force = rows(*forces)
        force_hi = force.astype(bf16).astype(f32)
        src = rows(force_hi, force - force_hi).astype(bf16)
        adj = dot(wreadt[...], src)
        a4[q] = adj
        put(s4s, q, adj.astype(bf16) * g4[q])
        return total

    total = lax.fori_loop(0, 8, top_step, within, unroll=8)

    psend[...] = total
    pl.semaphore_wait(far_sem, 2)
    sums = [
        remote(psend, pbuf.at[k], ps_sem.at[k], pr_sem.at[k], k) for k in range(1, blk)
    ]
    for copy in sums:
        copy.start()

    def back_step(q, carry):
        adj = a4[q] + dot(wb4[...], window(s4s, q))
        a3[q] = adj
        put(s3s, q, adj.astype(bf16) * g3[q])
        return carry

    lax.fori_loop(0, 8, back_step, 0, unroll=8)

    def low_step(q, carry):
        adj2 = a3[q] + dot(wb3[...], window(s3s, q))
        own, pushed = [], []
        for m in range(2):
            cols = slice(128 * m, 128 * m + 128)
            adj = lanes(adj2[0:64, cols], adj2[64:128, cols])
            own.append(adj)
            scaled = adj.astype(bf16) * g2[q, m]
            pushed.append(dot(wb2[...], scaled))
        adj1 = [
            pushed[0][0:64], pushed[1][0:64],
            own[0] + pushed[0][64:128], own[1] + pushed[1][64:128],
            pushed[0][128:192], pushed[1][128:192],
        ]
        src = []
        for j in range(6):
            adj = adj1[j].astype(bf16)
            src += [adj * g1[q, 64 * j:64 * j + 64], adj]
        a1s[q] = rows(*src)
        return carry

    lax.fori_loop(0, 8, low_step, 0, unroll=8)

    def lift_step(q, carry):
        both = dot(wb1[...], a1s[q])
        part = both[0:64] + both[64:128]
        for i in range(2):
            l = 2 * q + i
            cols = slice(128 * i, 128 * i + 128)
            gs_l[l] = part[8:24, cols].astype(bf16)
            gs_r[l] = part[40:56, cols].astype(bf16)
            for m in range(2):
                grad[m, l] += part[24 + 8 * m:32 + 8 * m, cols]
        gs_ll[q] = rows(part[0:8, 0:128], part[0:8, 128:256]).astype(bf16)
        gs_rr[q] = rows(part[56:64, 0:128], part[56:64, 128:256]).astype(bf16)
        return carry

    def back_part(n, k, src, dst, part, size):
        at = pl.ds(part * size, size)
        return remote(src.at[at], dst.at[at], gs_sem.at[n, part], gr_sem.at[n, part], k)

    back = [
        [
            back_part(2, 2, gs_rr, gr_ll, part, 2),
            back_part(3, -2, gs_ll, gr_rr, part, 2),
            back_part(0, 1, gs_r, gr_l, part, 4),
            back_part(1, -1, gs_l, gr_r, part, 4),
        ]
        for part in range(4)
    ]
    for part in range(4):
        lax.fori_loop(2 * part, 2 * part + 2, lift_step, 0, unroll=2)
        for copy in back[part]:
            copy.start()

    for copy in sums:
        copy.wait_recv()
    tile = psend[...]
    for k in range(1, blk):
        tile = tile + pbuf[k]
    full = jnp.sum(jnp.sum(tile, axis=1, keepdims=True), axis=0, keepdims=True)
    norm = jnp.sqrt(full / month_ref.size + 1e-05)
    scale = jnp.broadcast_to(step_size / norm, (8, 128))

    for q in range(8):
        if q % 2 == 0:
            for copy in back[q // 2]:
                copy.wait_recv()
        far_l = gr_ll[q].astype(f32) * has_ll
        far_r = gr_rr[q].astype(f32) * has_rr
        for i in range(2):
            l = 2 * q + i
            near = gr_l[l].astype(f32) * has_l + gr_r[l].astype(f32) * has_r
            far = (far_l[8 * i:8 * i + 8], far_r[8 * i:8 * i + 8])
            for m in range(2):
                g = grad[m, l] + near[8 * m:8 * m + 8] + far[m]
                out_ref[m, l] = base[m, l] - scale * g

    for copy in sum(halo + back, sums):
        copy.wait_send()


def shards(
    blk,
    sample, fresh_noise, proxy_month, proxy_cell, proxy_var, observed, proxy_weight,
    lift_weight, month_kernels, grid_kernels, read_weight,
):
    def grid(x):
        return x.reshape(32, 128)

    vmem = pltpu.VMEM
    dma = pltpu.SemaphoreType.DMA
    scratch = [
        vmem(sample.shape, f32), vmem(sample.shape, f32),
        vmem((32, 128), jnp.int32), vmem((32, 128), jnp.int32), vmem((32, 128), jnp.int32),
        vmem((32, 128), f32), vmem((32, 128), f32),
        vmem((8, 64), bf16), vmem(month_kernels.shape, bf16), vmem(grid_kernels.shape, bf16),
        vmem((8, 64), bf16),
        vmem((16, 16, 128), bf16), vmem((8, 16, 128), bf16), vmem((8, 16, 128), bf16),
        vmem((16, 16, 128), bf16), vmem((16, 16, 128), bf16),
        vmem((8, 16, 128), bf16), vmem((8, 16, 128), bf16),
        vmem((768, 256), bf16), vmem((64, 192), bf16),
        vmem((128, 768), bf16), vmem((128, 768), bf16), vmem((128, 768), bf16), vmem((128, 768), bf16),
        vmem((192, 64), bf16), vmem((128, 768), bf16),
        vmem((16, 128), bf16), vmem((128, 32), bf16),
        vmem((256, 512), f32),
        vmem((8, 384, 256), bf16), vmem((8, 128, 256), bf16), vmem((8, 768, 256), bf16),
        vmem((8, 384, 256), bf16), vmem((8, 2, 64, 256), bf16), vmem((8, 128, 256), bf16),
        vmem((8, 128, 256), bf16),
        vmem((3, 18, 64, 256), bf16), vmem((3, 18, 64, 256), bf16),
        vmem((3, 18, 64, 256), bf16), vmem((3, 18, 64, 256), bf16),
        vmem((8, 128, 256), f32), vmem((8, 128, 256), f32),
        vmem((2, 16, 8, 128), f32), vmem((2, 16, 8, 128), f32),
        vmem((16, 16, 128), bf16), vmem((16, 16, 128), bf16),
        vmem((8, 16, 128), bf16), vmem((8, 16, 128), bf16),
        vmem((16, 16, 128), bf16), vmem((16, 16, 128), bf16),
        vmem((8, 16, 128), bf16), vmem((8, 16, 128), bf16),
        vmem((8, 128), f32), vmem((blk, 8, 128), f32),
        dma((4, 4)), dma((4, 4)), dma((4, 4)), dma((4, 4)), dma((blk,)), dma((blk,)), dma((11,)),
        pltpu.SemaphoreType.REGULAR, pltpu.SemaphoreType.REGULAR,
    ]
    return pl.pallas_call(
        functools.partial(kernel, blk),
        out_shape=jax.ShapeDtypeStruct(sample.shape, f32),
        in_specs=[pl.BlockSpec(memory_space=pl.ANY)] * 11,
        out_specs=pl.BlockSpec(memory_space=pltpu.VMEM),
        scratch_shapes=scratch,
        compiler_params=pltpu.CompilerParams(collective_id=0, has_side_effects=True, vmem_limit_bytes=32 * 1024 * 1024),
        name="guided_step",
    )(*[pltpu.with_memory_space_constraint(x, pltpu.HBM) for x in (
        sample, fresh_noise, grid(proxy_month), grid(proxy_cell), grid(proxy_var),
        grid(observed), grid(proxy_weight), lift_weight.T, month_kernels, grid_kernels, read_weight,
    )])


def solution(mesh):
    in_specs = (
        P(("win", "blk"), None, None, None),
        P(("win", "blk"), None, None, None),
        P("win"),
        P("win"),
        P("win"),
        P("win"),
        P("win"),
        P(),
        P(),
        P(),
        P(),
    )
    out_specs = P(("win", "blk"), None, None, None)
    return jax.shard_map(
        functools.partial(shards, mesh.shape["blk"]),
        mesh=mesh, in_specs=in_specs, out_specs=out_specs, check_vma=False,
    )
```

```python
import functools

import jax
import jax.numpy as jnp
from jax import lax
from jax.experimental import pallas as pl
from jax.experimental.pallas import tpu as pltpu
from jax.sharding import PartitionSpec as P

tweedie_gain = 0.5
step_size = 0.25
guide_gain = 4.0
noise_gain = 0.5**0.5

f32 = jnp.float32
bf16 = jnp.bfloat16
MESH = pl.DeviceIdType.MESH

gelu_c = 0.7978845608028654
gelu_ca = gelu_c * 0.044715


def gelu_parts(x):
    x2 = x * x
    u = x * (gelu_c + gelu_ca * x2)
    h = 0.5 * jnp.tanh(u) + 0.5
    g = x * h
    dg = h + (g - g * h) * (2.0 * gelu_c + 6.0 * gelu_ca * x2)
    return g, dg


def dot(a, b):
    return jnp.dot(a, b, preferred_element_type=f32)


def dot_nt(a, b):
    return lax.dot_general(a, b, (((1,), (1,)), ((), ())), preferred_element_type=f32)


def lanes(*parts):
    return jnp.concatenate(parts, axis=1)


def rows(*parts):
    return jnp.concatenate(parts, axis=0)


def grid_weights(block):
    zero = jnp.zeros((64, 64), f32)
    upper, lower = [], []
    for b in range(3):
        taps = [block(a, b) for a in range(3)]
        upper += taps + [zero]
        lower += [zero] + taps
    return rows(lanes(*upper), lanes(*lower)).astype(bf16)


def grid_weights_tall(block):
    zero = jnp.zeros((64, 64), f32)
    taps = []
    for b in range(3):
        k = [block(a, b) for a in range(3)]
        taps.append(rows(lanes(*k, zero), lanes(zero, *k)))
    return rows(*[taps[b][16 * g:16 * g + 16] for g in range(8) for b in range(3)]).astype(bf16)


def lon_sum(out, first, last):
    groups = []
    for g in range(8):
        halves = []
        for m in range(2):
            tap = [out[48 * g + 16 * b:48 * g + 16 * b + 16, 128 * m:128 * m + 128] for b in range(3)]
            left = jnp.where(first, 0.0, pltpu.roll(tap[0], 1, 1))
            right = jnp.where(last, 0.0, pltpu.roll(tap[2], 127, 1))
            halves.append(tap[1] + left + right)
        groups.append(lanes(*halves))
    return rows(*groups)


def kernel(
    blk,
    sample_in, noise_in, month_in, cell_in, var_in, obs_in, pw_in,
    lift_in, mk_in, gk_in, read_in,
    out_ref,
    sample_ref, noise_ref, month_ref, cell_ref, var_ref, obs_ref, pw_ref,
    lift_ref, mk_ref, gk_ref, read_ref,
    send_pair, send_lo, send_hi, halo_l, halo_r, halo_ll, halo_rr,
    wf1, wf2, wf3, wf4, wb4, wb3, wb2, wb1, wread, wreadt,
    field,
    f4s, h1s, h4s, a1s, g1, g2, g3, g4, h2s, h3s, s4s, s3s, a4, a3,
    base, grad,
    gs_l, gs_r, gs_ll, gs_rr, gr_l, gr_r, gr_ll, gr_rr,
    psend, pbuf,
    hs_sem, hr_sem, gs_sem, gr_sem, ps_sem, pr_sem, in_sem, near_sem, far_sem,
):
    me = lax.axis_index("blk")

    def peer(k):
        return lax.rem(me + k + blk, blk)

    def remote(src, dst, ssem, rsem, k):
        return pltpu.make_async_remote_copy(
            src_ref=src, dst_ref=dst, send_sem=ssem, recv_sem=rsem,
            device_id={"blk": peer(k)}, device_id_type=MESH,
        )

    def signal(sem, k):
        pl.semaphore_signal(sem, inc=1, device_id={"blk": peer(k)}, device_id_type=MESH)

    barrier = pltpu.get_barrier_semaphore()
    for k in (2, -2, 1, -1):
        signal(barrier, k)

    loads = [
        pltpu.make_async_copy(src, dst, in_sem.at[n])
        for n, (src, dst) in enumerate((
            (sample_in, sample_ref), (mk_in, mk_ref), (lift_in, lift_ref), (gk_in, gk_ref),
            (read_in, read_ref), (month_in, month_ref), (cell_in, cell_ref), (var_in, var_ref),
            (obs_in, obs_ref), (pw_in, pw_ref), (noise_in, noise_ref),
        ))
    ]
    for copy in loads:
        copy.start()
    loads[0].wait()

    for l in range(16):
        send_pair[l] = rows(sample_ref[0, l], sample_ref[1, l]).astype(bf16)
    for q in range(8):
        send_lo[q] = rows(sample_ref[0, 2 * q], sample_ref[0, 2 * q + 1]).astype(bf16)
        send_hi[q] = rows(sample_ref[1, 2 * q], sample_ref[1, 2 * q + 1]).astype(bf16)

    pl.semaphore_wait(barrier, 4)

    def halo_part(n, k, src, dst, part, size):
        at = pl.ds(part * size, size)
        return remote(src.at[at], dst.at[at], hs_sem.at[n, part], hr_sem.at[n, part], k)

    halo = [
        [
            halo_part(2, 2, send_hi, halo_ll, part, 2),
            halo_part(3, -2, send_lo, halo_rr, part, 2),
            halo_part(0, 1, send_pair, halo_l, part, 4),
            halo_part(1, -1, send_pair, halo_r, part, 4),
        ]
        for part in range(4)
    ]
    for part in halo:
        for copy in part:
            copy.start()
    for k in (2, -2):
        signal(near_sem, k)
    for copy in loads[1:10]:
        copy.wait()

    has_l = jnp.where(me > 0, 1.0, 0.0).astype(f32)
    has_ll = jnp.where(me > 1, 1.0, 0.0).astype(f32)
    has_r = jnp.where(me < blk - 1, 1.0, 0.0).astype(f32)
    has_rr = jnp.where(me < blk - 2, 1.0, 0.0).astype(f32)

    lift = lift_ref[...]
    pick = (lax.broadcasted_iota(jnp.int32, (8, 64), 1) % 8
            == lax.broadcasted_iota(jnp.int32, (8, 64), 0))
    pick = jnp.where(pick, 1.0, 0.0).astype(bf16)
    tiled = lax.dot_general(
        lift, pick, (((0,), (0,)), ((), ())), preferred_element_type=f32
    )
    col_month = lax.broadcasted_iota(jnp.int32, (64, 64), 1) // 8
    placed = [jnp.where(col_month == i, tiled, 0.0) for i in range(8)]
    placed_b = [x.astype(bf16) for x in placed]
    inner_rows = []
    for j in range(6):
        acc = dot(mk_ref[0, 0], placed_b[j])
        acc = acc + dot(mk_ref[0, 1], placed_b[j + 1])
        acc = acc + dot(mk_ref[0, 2], placed_b[j + 2])
        inner_rows.append(acc)
    both = rows(*[x for j in range(6) for x in (inner_rows[j], placed[j + 1])])
    both_hi = both.astype(bf16).astype(f32)
    both_lo = both - both_hi
    wf1[...] = lanes(both_hi, both_lo, both_hi, jnp.zeros_like(both)).astype(bf16)
    flipped_hi = jnp.transpose(both_hi)
    flipped_lo = jnp.transpose(both_lo)
    wb1[...] = rows(flipped_hi, flipped_lo).astype(bf16)

    def mk(k):
        return mk_ref[1, k].astype(f32)

    wf2[...] = lanes(mk(0) * has_l, mk(1), mk(2) * has_r).astype(bf16)
    wb2[...] = rows(
        jnp.transpose(mk(0)) * has_l, jnp.transpose(mk(1)), jnp.transpose(mk(2)) * has_r
    ).astype(bf16)
    wf3[...] = grid_weights(lambda a, b: gk_ref[0, a, b].astype(f32))
    wf4[...] = grid_weights(lambda a, b: gk_ref[1, a, b].astype(f32))
    wb3[...] = grid_weights_tall(lambda a, b: jnp.transpose(gk_ref[0, 2 - a, 2 - b].astype(f32)))
    wb4[...] = grid_weights_tall(lambda a, b: jnp.transpose(gk_ref[1, 2 - a, 2 - b].astype(f32)))
    read = read_ref[...].astype(f32)
    zero_read = jnp.zeros((8, 64), f32)
    wide = rows(lanes(read, zero_read), lanes(zero_read, read))
    wread[...] = wide.astype(bf16)
    tall = jnp.transpose(wide)
    wreadt[...] = lanes(tall, tall).astype(bf16)

    local = month_ref[...] - 2 * me
    owned = jnp.logical_and(local >= 0, local < 2)
    cell = cell_ref[...]
    row_of = jnp.where(owned, (local * 16 + lax.shift_right_logical(cell, 7)) * 8 + var_ref[...], -1)
    lon_of = jnp.bitwise_and(cell, 127)
    weight = pw_ref[...]
    weighted = weight * obs_ref[...]
    w_hi = weight.astype(bf16).astype(f32)
    w_lo = (weight - w_hi).astype(bf16).astype(f32)
    b_hi = weighted.astype(bf16).astype(f32)
    b_lo = (weighted - b_hi).astype(bf16).astype(f32)
    b_sum = b_hi + b_lo
    spread_terms = jnp.where(owned, b_sum * b_sum / (w_hi + w_lo), 0.0)
    within = (spread_terms[0:8] + spread_terms[8:16]) + (spread_terms[16:24] + spread_terms[24:32])
    row_iota = lax.broadcasted_iota(jnp.int32, (256, 128), 0)
    lon_iota = lax.broadcasted_iota(jnp.int32, (128, 128), 0)
    for c in range(4):
        lhs, rhs = [], []
        for r in range(8 * c, 8 * c + 8):
            lhs.append(jnp.where(row_iota == row_of[r:r + 1], 1.0, 0.0).astype(bf16))
            at = lon_iota == lon_of[r:r + 1]
            rhs.append(rows(*[
                jnp.where(at, x[r:r + 1], 0.0).astype(bf16) for x in (w_hi, w_lo, b_hi, b_lo)
            ]))
        part = dot_nt(lanes(*lhs), lanes(*rhs))
        if c == 0:
            field[...] = part
        else:
            field[...] += part
    w_field = field[:, 0:128] + field[:, 128:256]
    b_field = field[:, 256:384] + field[:, 384:512]
    mean = jnp.where(w_field > 0.0, b_field / jnp.where(w_field > 0.0, w_field, 1.0), 0.0)
    field[:, 0:128] = w_field
    field[:, 128:256] = mean
    taken = b_field * mean
    for r in range(32):
        within = within - taken[8 * r:8 * r + 8]

    zero_row = jnp.zeros((64, 256), bf16)
    for ref in (s4s, s3s):
        ref[0] = zero_row
        ref[17] = zero_row
    for ref in (h2s, h3s):
        for tap in range(3):
            ref[tap, 0] = zero_row
            ref[tap, 17] = zero_row

    lane = lax.broadcasted_iota(jnp.int32, (128, 128), 1)
    first, last = lane == 0, lane == 127
    lane16 = lax.broadcasted_iota(jnp.int32, (16, 128), 1)
    first16, last16 = lane16 == 0, lane16 == 127
    zero_half = jnp.zeros((128, 128), bf16)

    def window(ref, q):
        return rows(*[ref[tap, pl.ds(2 * q, 4)].reshape(256, 256) for tap in range(3)])

    def rows4(ref, q):
        return ref[pl.ds(2 * q, 4)].reshape(256, 256)

    def pair(ref, q):
        return ref[1, pl.ds(2 * q + 1, 2)].reshape(128, 256)

    def put(ref, q, value):
        left, right = [], []
        for m in range(2):
            half = value[:, 128 * m:128 * m + 128]
            left.append(jnp.where(first, zero_half, pltpu.roll(half, 1, 1)))
            right.append(jnp.where(last, zero_half, pltpu.roll(half, 127, 1)))
        at = pl.ds(2 * q + 1, 2)
        ref[0, at] = lanes(*left).reshape(2, 64, 256)
        ref[1, at] = value.reshape(2, 64, 256)
        ref[2, at] = lanes(*right).reshape(2, 64, 256)

    def month_step(q, carry):
        highs, lows = [], []
        for i in range(2):
            l = 2 * q + i
            prev = halo_l[l].astype(f32) * has_l
            nxt = halo_r[l].astype(f32) * has_r
            prev2 = halo_ll[q].astype(f32)[8 * i:8 * i + 8] * has_ll
            nxt2 = halo_rr[q].astype(f32)[8 * i:8 * i + 8] * has_rr
            own = rows(sample_ref[0, l], sample_ref[1, l])
            own_hi = own.astype(bf16).astype(f32)
            highs.append(rows(prev2, prev, own_hi, nxt, nxt2))
            z = jnp.zeros((24, 128), f32)
            lows.append(rows(z, own - own_hi, z))
        high = lanes(*highs)
        src = rows(high, high, lanes(*lows), jnp.zeros((64, 256), f32)).astype(bf16)
        out = dot(wf1[...], src).astype(bf16)
        hidden = []
        for j in range(6):
            gel, der = gelu_parts(out[128 * j:128 * j + 64])
            g1[q, 64 * j:64 * j + 64] = der
            hidden.append(out[128 * j + 64:128 * j + 128] + gel)
        h1s[q] = rows(*hidden)
        return carry

    def month_step2(q, carry):
        halves = []
        for m in range(2):
            src2 = rows(*[h1s[q, 64 * j:64 * j + 64] for j in (m, m + 2, m + 4)])
            gel2, der2 = gelu_parts(dot(wf2[...], src2).astype(bf16))
            g2[q, m] = der2
            nxt_h = h1s[q, 64 * (m + 2):64 * (m + 3)] + gel2
            halves.append(rows(nxt_h[:, 0:128], nxt_h[:, 128:256]))
        put(h2s, q, lanes(*halves))
        return carry


    def grid_step(q, carry):
        inner = dot(wf3[...], window(h2s, q)).astype(bf16)
        gel, der = gelu_parts(inner)
        g3[q] = der
        put(h3s, q, pair(h2s, q) + gel)
        return carry


    def last_step(q, carry):
        inner = dot(wf4[...], window(h3s, q)).astype(bf16)
        gel, der = gelu_parts(inner)
        g4[q] = der
        h4s[q] = pair(h3s, q) + gel
        return carry


    def top_step(q, total):
        score = dot(wread[...], h4s[q])
        forces = []
        for i in range(2):
            l = 2 * q + i
            line = []
            for m in range(2):
                sc = score[8 * i:8 * i + 8, 128 * m:128 * m + 128]
                sm = sample_ref[m, l]
                at = pl.ds((m * 16 + l) * 8, 8)
                w = field[at, 0:128]
                delta = sm + tweedie_gain * sc - field[at, 128:256]
                pull = w * delta
                total = total + pull * delta
                force = guide_gain * pull
                base[m, l] = sm + step_size * sc + noise_gain * noise_ref[m, l]
                grad[m, l] = force
                line.append(tweedie_gain * force)
            forces.append(lanes(*line))
        force = rows(*forces)
        force_hi = force.astype(bf16).astype(f32)
        f4s[q] = rows(force_hi, force - force_hi).astype(bf16)
        return total

    def adjoint_step(q, carry):
        adj = dot(wreadt[...], f4s[q])
        a4[q] = adj
        s4s[pl.ds(2 * q + 1, 2)] = (adj.astype(bf16) * g4[q]).reshape(2, 64, 256)
        return carry

    def run(step, part, carry=0):
        return lax.fori_loop(2 * part, 2 * part + 2, step, carry, unroll=2)

    pl.semaphore_wait(near_sem, 2)
    for k in (4, -4):
        signal(far_sem, k)
    loads[10].wait()
    total = within
    for part in range(4):
        for copy in halo[part]:
            copy.wait_recv()
        run(month_step, part)
    lax.fori_loop(0, 8, month_step2, 0, unroll=8)
    lax.fori_loop(0, 8, grid_step, 0, unroll=8)
    lax.fori_loop(0, 8, last_step, 0, unroll=8)
    total = lax.fori_loop(0, 8, top_step, total, unroll=8)

    psend[...] = total
    pl.semaphore_wait(far_sem, 2)
    sums = [
        remote(psend, pbuf.at[k], ps_sem.at[k], pr_sem.at[k], k) for k in range(1, blk)
    ]
    for copy in sums:
        copy.start()
    lax.fori_loop(0, 8, adjoint_step, 0, unroll=8)

    def back_step(q, carry):
        adj = a4[q] + lon_sum(dot(wb4[...], rows4(s4s, q)), first16, last16)
        a3[q] = adj
        s3s[pl.ds(2 * q + 1, 2)] = (adj.astype(bf16) * g3[q]).reshape(2, 64, 256)
        return carry


    def low_step(q, carry):
        adj2 = a3[q] + lon_sum(dot(wb3[...], rows4(s3s, q)), first16, last16)
        own, pushed = [], []
        for m in range(2):
            cols = slice(128 * m, 128 * m + 128)
            adj = lanes(adj2[0:64, cols], adj2[64:128, cols])
            own.append(adj)
            scaled = adj.astype(bf16) * g2[q, m]
            pushed.append(dot(wb2[...], scaled))
        adj1 = [
            pushed[0][0:64], pushed[1][0:64],
            own[0] + pushed[0][64:128], own[1] + pushed[1][64:128],
            pushed[0][128:192], pushed[1][128:192],
        ]
        src = []
        for j in range(6):
            adj = adj1[j].astype(bf16)
            src += [adj * g1[q, 64 * j:64 * j + 64], adj]
        a1s[q] = rows(*src)
        return carry


    def lift_step(q, carry):
        both = dot(wb1[...], a1s[q])
        part = both[0:64] + both[64:128]
        for i in range(2):
            l = 2 * q + i
            cols = slice(128 * i, 128 * i + 128)
            gs_l[l] = part[8:24, cols].astype(bf16)
            gs_r[l] = part[40:56, cols].astype(bf16)
            for m in range(2):
                grad[m, l] += part[24 + 8 * m:32 + 8 * m, cols]
        gs_ll[q] = rows(part[0:8, 0:128], part[0:8, 128:256]).astype(bf16)
        gs_rr[q] = rows(part[56:64, 0:128], part[56:64, 128:256]).astype(bf16)
        return carry

    def back_part(n, k, src, dst, part, size):
        at = pl.ds(part * size, size)
        return remote(src.at[at], dst.at[at], gs_sem.at[n, part], gr_sem.at[n, part], k)

    back = [
        [
            back_part(2, 2, gs_rr, gr_ll, part, 2),
            back_part(3, -2, gs_ll, gr_rr, part, 2),
            back_part(0, 1, gs_r, gr_l, part, 4),
            back_part(1, -1, gs_l, gr_r, part, 4),
        ]
        for part in range(4)
    ]
    for wave in range(6):
        if wave == 0:
            run(back_step, 0)
        if wave + 1 < 4:
            run(back_step, wave + 1)
        if 0 <= wave - 1 < 4:
            run(low_step, wave - 1)
        if 0 <= wave - 2 < 4:
            run(lift_step, wave - 2)
            for copy in back[wave - 2]:
                copy.start()

    for copy in sums:
        copy.wait_recv()
    tile = psend[...]
    for k in range(1, blk):
        tile = tile + pbuf[k]
    full = jnp.sum(jnp.sum(tile, axis=1, keepdims=True), axis=0, keepdims=True)
    norm = jnp.sqrt(full / month_ref.size + 1e-05)
    scale = jnp.broadcast_to(step_size / norm, (8, 128))

    for q in range(8):
        if q % 2 == 0:
            for copy in back[q // 2]:
                copy.wait_recv()
        far_l = gr_ll[q].astype(f32) * has_ll
        far_r = gr_rr[q].astype(f32) * has_rr
        for i in range(2):
            l = 2 * q + i
            near = gr_l[l].astype(f32) * has_l + gr_r[l].astype(f32) * has_r
            far = (far_l[8 * i:8 * i + 8], far_r[8 * i:8 * i + 8])
            for m in range(2):
                g = grad[m, l] + near[8 * m:8 * m + 8] + far[m]
                out_ref[m, l] = base[m, l] - scale * g

    for copy in sum(halo + back, sums):
        copy.wait_send()


def shards(
    blk,
    sample, fresh_noise, proxy_month, proxy_cell, proxy_var, observed, proxy_weight,
    lift_weight, month_kernels, grid_kernels, read_weight,
):
    def grid(x):
        return x.reshape(32, 128)

    vmem = pltpu.VMEM
    dma = pltpu.SemaphoreType.DMA
    scratch = [
        vmem(sample.shape, f32), vmem(sample.shape, f32),
        vmem((32, 128), jnp.int32), vmem((32, 128), jnp.int32), vmem((32, 128), jnp.int32),
        vmem((32, 128), f32), vmem((32, 128), f32),
        vmem((8, 64), bf16), vmem(month_kernels.shape, bf16), vmem(grid_kernels.shape, bf16),
        vmem((8, 64), bf16),
        vmem((16, 16, 128), bf16), vmem((8, 16, 128), bf16), vmem((8, 16, 128), bf16),
        vmem((16, 16, 128), bf16), vmem((16, 16, 128), bf16),
        vmem((8, 16, 128), bf16), vmem((8, 16, 128), bf16),
        vmem((768, 256), bf16), vmem((64, 192), bf16),
        vmem((128, 768), bf16), vmem((128, 768), bf16), vmem((384, 256), bf16), vmem((384, 256), bf16),
        vmem((192, 64), bf16), vmem((128, 768), bf16),
        vmem((16, 128), bf16), vmem((128, 32), bf16),
        vmem((256, 512), f32),
        vmem((8, 32, 256), bf16),
        vmem((8, 384, 256), bf16), vmem((8, 128, 256), bf16), vmem((8, 768, 256), bf16),
        vmem((8, 384, 256), bf16), vmem((8, 2, 64, 256), bf16), vmem((8, 128, 256), bf16),
        vmem((8, 128, 256), bf16),
        vmem((3, 18, 64, 256), bf16), vmem((3, 18, 64, 256), bf16),
        vmem((18, 64, 256), bf16), vmem((18, 64, 256), bf16),
        vmem((8, 128, 256), f32), vmem((8, 128, 256), f32),
        vmem((2, 16, 8, 128), f32), vmem((2, 16, 8, 128), f32),
        vmem((16, 16, 128), bf16), vmem((16, 16, 128), bf16),
        vmem((8, 16, 128), bf16), vmem((8, 16, 128), bf16),
        vmem((16, 16, 128), bf16), vmem((16, 16, 128), bf16),
        vmem((8, 16, 128), bf16), vmem((8, 16, 128), bf16),
        vmem((8, 128), f32), vmem((blk, 8, 128), f32),
        dma((4, 4)), dma((4, 4)), dma((4, 4)), dma((4, 4)), dma((blk,)), dma((blk,)), dma((11,)),
        pltpu.SemaphoreType.REGULAR, pltpu.SemaphoreType.REGULAR,
    ]
    return pl.pallas_call(
        functools.partial(kernel, blk),
        out_shape=jax.ShapeDtypeStruct(sample.shape, f32),
        in_specs=[pl.BlockSpec(memory_space=pl.ANY)] * 11,
        out_specs=pl.BlockSpec(memory_space=pltpu.VMEM),
        scratch_shapes=scratch,
        compiler_params=pltpu.CompilerParams(collective_id=0, has_side_effects=True, vmem_limit_bytes=32 * 1024 * 1024),
        name="guided_step",
    )(*[pltpu.with_memory_space_constraint(x, pltpu.HBM) for x in (
        sample, fresh_noise, grid(proxy_month), grid(proxy_cell), grid(proxy_var),
        grid(observed), grid(proxy_weight), lift_weight.T, month_kernels, grid_kernels, read_weight,
    )])


def solution(mesh):
    in_specs = (
        P(("win", "blk"), None, None, None),
        P(("win", "blk"), None, None, None),
        P("win"),
        P("win"),
        P("win"),
        P("win"),
        P("win"),
        P(),
        P(),
        P(),
        P(),
    )
    out_specs = P(("win", "blk"), None, None, None)
    return jax.shard_map(
        functools.partial(shards, mesh.shape["blk"]),
        mesh=mesh, in_specs=in_specs, out_specs=out_specs, check_vma=False,
    )
```

```python
import functools

import jax
import jax.numpy as jnp
from jax import lax
from jax.experimental import pallas as pl
from jax.experimental.pallas import tpu as pltpu
from jax.sharding import PartitionSpec as P

tweedie_gain = 0.5
step_size = 0.25
guide_gain = 4.0
noise_gain = 0.5**0.5

f32 = jnp.float32
bf16 = jnp.bfloat16
MESH = pl.DeviceIdType.MESH

gelu_c = 0.7978845608028654
gelu_ca = gelu_c * 0.044715


def gelu_parts(x):
    x2 = x * x
    u = x * (gelu_c + gelu_ca * x2)
    h = 0.5 * jnp.tanh(u) + 0.5
    g = x * h
    dg = h + (g - g * h) * (2.0 * gelu_c + 6.0 * gelu_ca * x2)
    return g, dg


def dot(a, b):
    return jnp.dot(a, b, preferred_element_type=f32)


def dot_nt(a, b):
    return lax.dot_general(a, b, (((1,), (1,)), ((), ())), preferred_element_type=f32)


def lanes(*parts):
    return jnp.concatenate(parts, axis=1)


def rows(*parts):
    return jnp.concatenate(parts, axis=0)


def grid_weights(block):
    zero = jnp.zeros((64, 64), f32)
    upper, lower = [], []
    for b in range(3):
        taps = [block(a, b) for a in range(3)]
        upper += taps + [zero]
        lower += [zero] + taps
    return rows(lanes(*upper), lanes(*lower)).astype(bf16)


def grid_weights_tall(block):
    zero = jnp.zeros((64, 64), f32)
    taps = []
    for b in range(3):
        k = [block(a, b) for a in range(3)]
        taps.append(rows(lanes(*k, zero), lanes(zero, *k)))
    return rows(*[taps[b][16 * g:16 * g + 16] for g in range(8) for b in range(3)]).astype(bf16)


def lon_sum(out, first, last):
    groups = []
    for g in range(8):
        halves = []
        for m in range(2):
            tap = [out[48 * g + 16 * b:48 * g + 16 * b + 16, 128 * m:128 * m + 128] for b in range(3)]
            left = jnp.where(first, 0.0, pltpu.roll(tap[0], 1, 1))
            right = jnp.where(last, 0.0, pltpu.roll(tap[2], 127, 1))
            halves.append(tap[1] + left + right)
        groups.append(lanes(*halves))
    return rows(*groups)


def kernel(
    blk,
    sample_in, noise_in, month_in, cell_in, var_in, obs_in, pw_in,
    lift_in, mk_in, gk_in, read_in,
    out_ref,
    sample_ref, noise_ref, month_ref, cell_ref, var_ref, obs_ref, pw_ref,
    lift_ref, mk_ref, gk_ref, read_ref,
    send_pair, send_lo, send_hi, halo_l, halo_r, halo_ll, halo_rr,
    wf1, wf2, wf3, wf4, wb4, wb3, wb2, wb1, wread, wreadt,
    field,
    f4s, h1s, h4s, a1s, g1, g2, g3, g4, h2s, h3s, s4s, s3s, a4, a3,
    base, grad,
    gs_l, gs_r, gs_ll, gs_rr, gr_l, gr_r, gr_ll, gr_rr,
    psend, pbuf,
    hs_sem, hr_sem, gs_sem, gr_sem, ps_sem, pr_sem, in_sem, near_sem, far_sem, wide_sem,
):
    me = lax.axis_index("blk")

    def peer(k):
        return lax.rem(me + k + blk, blk)

    def remote(src, dst, ssem, rsem, k):
        return pltpu.make_async_remote_copy(
            src_ref=src, dst_ref=dst, send_sem=ssem, recv_sem=rsem,
            device_id={"blk": peer(k)}, device_id_type=MESH,
        )

    def there(k):
        return jnp.logical_and(me + k >= 0, me + k < blk)

    def count(*ks):
        return sum(jnp.where(there(k), 1, 0) for k in ks)

    def signal(sem, k):
        @pl.when(there(k))
        def _():
            pl.semaphore_signal(sem, inc=1, device_id={"blk": peer(k)}, device_id_type=MESH)

    class Link:
        def __init__(self, src, dst, ssem, rsem, k):
            self.copy, self.k = remote(src, dst, ssem, rsem, k), k

        def start(self):
            self.copy.start()

        def wait_send(self):
            self.copy.wait_send()

        def wait_recv(self):
            self.copy.wait_recv()

    inside = jnp.logical_and(me >= 2, me < blk - 2)

    def each(links, act, way):
        @pl.when(inside)
        def _():
            for link in links:
                act(link)

        @pl.when(jnp.logical_not(inside))
        def _():
            for link in links:
                pl.when(there(way * link.k))(functools.partial(act, link))

    def start_all(links):
        each(links, Link.start, 1)

    def sent_all(links):
        each(links, Link.wait_send, 1)

    def got_all(links):
        each(links, Link.wait_recv, -1)

    barrier = pltpu.get_barrier_semaphore()
    for k in (2, -2, 1, -1):
        signal(barrier, k)

    loads = [
        pltpu.make_async_copy(src, dst, in_sem.at[n])
        for n, (src, dst) in enumerate((
            (sample_in, sample_ref), (mk_in, mk_ref), (lift_in, lift_ref), (gk_in, gk_ref),
            (read_in, read_ref), (month_in, month_ref), (cell_in, cell_ref), (var_in, var_ref),
            (obs_in, obs_ref), (pw_in, pw_ref), (noise_in, noise_ref),
        ))
    ]
    for copy in loads:
        copy.start()
    loads[0].wait()

    for l in range(16):
        send_pair[l] = rows(sample_ref[0, l], sample_ref[1, l]).astype(bf16)
    for q in range(8):
        send_lo[q] = rows(sample_ref[0, 2 * q], sample_ref[0, 2 * q + 1]).astype(bf16)
        send_hi[q] = rows(sample_ref[1, 2 * q], sample_ref[1, 2 * q + 1]).astype(bf16)

    pl.semaphore_wait(barrier, count(1, -1, 2, -2))

    def halo_part(n, k, src, dst, part, size):
        at = pl.ds(part * size, size)
        return Link(src.at[at], dst.at[at], hs_sem.at[n, part], hr_sem.at[n, part], k)

    halo = [
        [
            halo_part(2, 2, send_hi, halo_ll, part, 4),
            halo_part(3, -2, send_lo, halo_rr, part, 4),
            halo_part(0, 1, send_pair, halo_l, part, 8),
            halo_part(1, -1, send_pair, halo_r, part, 8),
        ]
        for part in range(2)
    ]
    for part in halo:
        start_all(part)
    for k, bufs in ((-1, (halo_l, gr_l)), (1, (halo_r, gr_r)), (-2, (halo_ll, gr_ll)), (2, (halo_rr, gr_rr))):
        @pl.when(jnp.logical_not(there(k)))
        def _():
            for ref in bufs:
                ref[...] = jnp.zeros(ref.shape, bf16)
    for k in (2, -2):
        signal(near_sem, k)
    for copy in loads[1:10]:
        copy.wait()

    has_l = jnp.where(me > 0, 1.0, 0.0).astype(f32)
    has_r = jnp.where(me < blk - 1, 1.0, 0.0).astype(f32)

    lift = lift_ref[...]
    pick = (lax.broadcasted_iota(jnp.int32, (8, 64), 1) % 8
            == lax.broadcasted_iota(jnp.int32, (8, 64), 0))
    pick = jnp.where(pick, 1.0, 0.0).astype(bf16)
    tiled = lax.dot_general(
        lift, pick, (((0,), (0,)), ((), ())), preferred_element_type=f32
    )
    col_month = lax.broadcasted_iota(jnp.int32, (64, 64), 1) // 8
    placed = [jnp.where(col_month == i, tiled, 0.0) for i in range(8)]
    placed_b = [x.astype(bf16) for x in placed]
    inner_rows = []
    for j in range(6):
        acc = dot(mk_ref[0, 0], placed_b[j])
        acc = acc + dot(mk_ref[0, 1], placed_b[j + 1])
        acc = acc + dot(mk_ref[0, 2], placed_b[j + 2])
        inner_rows.append(acc)
    both = rows(*[x for j in range(6) for x in (inner_rows[j], placed[j + 1])])
    both_hi = both.astype(bf16).astype(f32)
    both_lo = both - both_hi
    wf1[...] = lanes(both_hi, both_lo, both_hi, jnp.zeros_like(both)).astype(bf16)
    flipped_hi = jnp.transpose(both_hi)
    flipped_lo = jnp.transpose(both_lo)
    wb1[...] = rows(flipped_hi, flipped_lo).astype(bf16)

    def mk(k):
        return mk_ref[1, k].astype(f32)

    wf2[...] = lanes(mk(0) * has_l, mk(1), mk(2) * has_r).astype(bf16)
    wb2[...] = rows(
        jnp.transpose(mk(0)) * has_l, jnp.transpose(mk(1)), jnp.transpose(mk(2)) * has_r
    ).astype(bf16)
    wf3[...] = grid_weights(lambda a, b: gk_ref[0, a, b].astype(f32))
    wf4[...] = grid_weights(lambda a, b: gk_ref[1, a, b].astype(f32))
    wb3[...] = grid_weights_tall(lambda a, b: jnp.transpose(gk_ref[0, 2 - a, 2 - b].astype(f32)))
    wb4[...] = grid_weights_tall(lambda a, b: jnp.transpose(gk_ref[1, 2 - a, 2 - b].astype(f32)))
    read = read_ref[...].astype(f32)
    zero_read = jnp.zeros((8, 64), f32)
    wide = rows(lanes(read, zero_read), lanes(zero_read, read))
    wread[...] = wide.astype(bf16)
    tall = jnp.transpose(wide)
    wreadt[...] = lanes(tall, tall).astype(bf16)

    local = month_ref[...] - 2 * me
    owned = jnp.logical_and(local >= 0, local < 2)
    cell = cell_ref[...]
    row_of = jnp.where(owned, (local * 16 + lax.shift_right_logical(cell, 7)) * 8 + var_ref[...], -1)
    lon_of = jnp.bitwise_and(cell, 127)
    weight = pw_ref[...]
    weighted = weight * obs_ref[...]
    w_hi = weight.astype(bf16).astype(f32)
    w_lo = (weight - w_hi).astype(bf16).astype(f32)
    b_hi = weighted.astype(bf16).astype(f32)
    b_lo = (weighted - b_hi).astype(bf16).astype(f32)
    b_sum = b_hi + b_lo
    spread_terms = jnp.where(owned, b_sum * b_sum / (w_hi + w_lo), 0.0)
    within = (spread_terms[0:8] + spread_terms[8:16]) + (spread_terms[16:24] + spread_terms[24:32])
    row_iota = lax.broadcasted_iota(jnp.int32, (256, 128), 0)
    lon_iota = lax.broadcasted_iota(jnp.int32, (128, 128), 0)
    for c in range(4):
        lhs, rhs = [], []
        for r in range(8 * c, 8 * c + 8):
            lhs.append(jnp.where(row_iota == row_of[r:r + 1], 1.0, 0.0).astype(bf16))
            at = lon_iota == lon_of[r:r + 1]
            rhs.append(rows(*[
                jnp.where(at, x[r:r + 1], 0.0).astype(bf16) for x in (w_hi, w_lo, b_hi, b_lo)
            ]))
        part = dot_nt(lanes(*lhs), lanes(*rhs))
        if c == 0:
            field[...] = part
        else:
            field[...] += part
    w_field = field[:, 0:128] + field[:, 128:256]
    b_field = field[:, 256:384] + field[:, 384:512]
    mean = jnp.where(w_field > 0.0, b_field / jnp.where(w_field > 0.0, w_field, 1.0), 0.0)
    field[:, 0:128] = w_field
    field[:, 128:256] = mean
    taken = b_field * mean
    for r in range(32):
        within = within - taken[8 * r:8 * r + 8]

    zero_row = jnp.zeros((64, 256), bf16)
    for ref in (s4s, s3s):
        ref[0] = zero_row
        ref[17] = zero_row
    for ref in (h2s, h3s):
        for tap in range(3):
            ref[tap, 0] = zero_row
            ref[tap, 17] = zero_row

    lane = lax.broadcasted_iota(jnp.int32, (128, 128), 1)
    first, last = lane == 0, lane == 127
    lane16 = lax.broadcasted_iota(jnp.int32, (16, 128), 1)
    first16, last16 = lane16 == 0, lane16 == 127
    zero_half = jnp.zeros((128, 128), bf16)

    def window(ref, q):
        return rows(*[ref[tap, pl.ds(2 * q, 4)].reshape(256, 256) for tap in range(3)])

    def rows4(ref, q):
        return ref[pl.ds(2 * q, 4)].reshape(256, 256)

    def pair(ref, q):
        return ref[1, pl.ds(2 * q + 1, 2)].reshape(128, 256)

    def put(ref, q, value):
        left, right = [], []
        for m in range(2):
            half = value[:, 128 * m:128 * m + 128]
            left.append(jnp.where(first, zero_half, pltpu.roll(half, 1, 1)))
            right.append(jnp.where(last, zero_half, pltpu.roll(half, 127, 1)))
        at = pl.ds(2 * q + 1, 2)
        ref[0, at] = lanes(*left).reshape(2, 64, 256)
        ref[1, at] = value.reshape(2, 64, 256)
        ref[2, at] = lanes(*right).reshape(2, 64, 256)

    def month_step(q, carry):
        highs, lows = [], []
        for i in range(2):
            l = 2 * q + i
            prev = halo_l[l].astype(f32)
            nxt = halo_r[l].astype(f32)
            prev2 = halo_ll[q].astype(f32)[8 * i:8 * i + 8]
            nxt2 = halo_rr[q].astype(f32)[8 * i:8 * i + 8]
            own = rows(sample_ref[0, l], sample_ref[1, l])
            own_hi = own.astype(bf16).astype(f32)
            highs.append(rows(prev2, prev, own_hi, nxt, nxt2))
            z = jnp.zeros((24, 128), f32)
            lows.append(rows(z, own - own_hi, z))
        high = lanes(*highs)
        src = rows(high, high, lanes(*lows), jnp.zeros((64, 256), f32)).astype(bf16)
        out = dot(wf1[...], src).astype(bf16)
        hidden = []
        for j in range(6):
            gel, der = gelu_parts(out[128 * j:128 * j + 64])
            g1[q, 64 * j:64 * j + 64] = der
            hidden.append(out[128 * j + 64:128 * j + 128] + gel)
        h1s[q] = rows(*hidden)
        return carry

    def month_step2(q, carry):
        halves = []
        for m in range(2):
            src2 = rows(*[h1s[q, 64 * j:64 * j + 64] for j in (m, m + 2, m + 4)])
            gel2, der2 = gelu_parts(dot(wf2[...], src2).astype(bf16))
            g2[q, m] = der2
            nxt_h = h1s[q, 64 * (m + 2):64 * (m + 3)] + gel2
            halves.append(rows(nxt_h[:, 0:128], nxt_h[:, 128:256]))
        put(h2s, q, lanes(*halves))
        return carry


    def grid_step(q, carry):
        inner = dot(wf3[...], window(h2s, q)).astype(bf16)
        gel, der = gelu_parts(inner)
        g3[q] = der
        put(h3s, q, pair(h2s, q) + gel)
        return carry


    def last_step(q, carry):
        inner = dot(wf4[...], window(h3s, q)).astype(bf16)
        gel, der = gelu_parts(inner)
        g4[q] = der
        h4s[q] = pair(h3s, q) + gel
        return carry


    def top_step(q, total):
        score = dot(wread[...], h4s[q])
        forces = []
        for i in range(2):
            l = 2 * q + i
            line = []
            for m in range(2):
                sc = score[8 * i:8 * i + 8, 128 * m:128 * m + 128]
                sm = sample_ref[m, l]
                at = pl.ds((m * 16 + l) * 8, 8)
                w = field[at, 0:128]
                delta = sm + tweedie_gain * sc - field[at, 128:256]
                pull = w * delta
                total = total + pull * delta
                force = guide_gain * pull
                base[m, l] = sm + step_size * sc + noise_gain * noise_ref[m, l]
                grad[m, l] = force
                line.append(tweedie_gain * force)
            forces.append(lanes(*line))
        force = rows(*forces)
        force_hi = force.astype(bf16).astype(f32)
        f4s[q] = rows(force_hi, force - force_hi).astype(bf16)
        return total

    def adjoint_step(q, carry):
        adj = dot(wreadt[...], f4s[q])
        a4[q] = adj
        s4s[pl.ds(2 * q + 1, 2)] = (adj.astype(bf16) * g4[q]).reshape(2, 64, 256)
        return carry

    def run(step, part, carry=0):
        return lax.fori_loop(2 * part, 2 * part + 2, step, carry, unroll=2)

    pl.semaphore_wait(near_sem, count(2, -2))
    for k in (4, -4):
        signal(far_sem, k)
    loads[10].wait()
    total = within
    for part in range(2):
        got_all(halo[part])
        lax.fori_loop(4 * part, 4 * part + 4, month_step, 0, unroll=4)
    pl.semaphore_wait(far_sem, count(4, -4))
    for k in (8, -8):
        signal(wide_sem, k)
    lax.fori_loop(0, 8, month_step2, 0, unroll=8)
    lax.fori_loop(0, 8, grid_step, 0, unroll=8)
    lax.fori_loop(0, 8, last_step, 0, unroll=8)
    total = lax.fori_loop(0, 8, top_step, total, unroll=8)

    psend[...] = jnp.sum(total, axis=0, keepdims=True)
    pl.semaphore_wait(wide_sem, count(8, -8))
    sums = [
        remote(psend, pbuf.at[k], ps_sem.at[k], pr_sem.at[k], k) for k in range(1, blk)
    ]
    for copy in sums:
        copy.start()
    lax.fori_loop(0, 8, adjoint_step, 0, unroll=8)

    def back_step(q, carry):
        adj = a4[q] + lon_sum(dot(wb4[...], rows4(s4s, q)), first16, last16)
        a3[q] = adj
        s3s[pl.ds(2 * q + 1, 2)] = (adj.astype(bf16) * g3[q]).reshape(2, 64, 256)
        return carry


    def low_step(q, carry):
        adj2 = a3[q] + lon_sum(dot(wb3[...], rows4(s3s, q)), first16, last16)
        own, pushed = [], []
        for m in range(2):
            cols = slice(128 * m, 128 * m + 128)
            adj = lanes(adj2[0:64, cols], adj2[64:128, cols])
            own.append(adj)
            scaled = adj.astype(bf16) * g2[q, m]
            pushed.append(dot(wb2[...], scaled))
        adj1 = [
            pushed[0][0:64], pushed[1][0:64],
            own[0] + pushed[0][64:128], own[1] + pushed[1][64:128],
            pushed[0][128:192], pushed[1][128:192],
        ]
        src = []
        for j in range(6):
            adj = adj1[j].astype(bf16)
            src += [adj * g1[q, 64 * j:64 * j + 64], adj]
        a1s[q] = rows(*src)
        return carry


    def lift_step(q, carry):
        both = dot(wb1[...], a1s[q])
        part = both[0:64] + both[64:128]
        for i in range(2):
            l = 2 * q + i
            cols = slice(128 * i, 128 * i + 128)
            gs_l[l] = part[8:24, cols].astype(bf16)
            gs_r[l] = part[40:56, cols].astype(bf16)
            for m in range(2):
                grad[m, l] += part[24 + 8 * m:32 + 8 * m, cols]
        gs_ll[q] = rows(part[0:8, 0:128], part[0:8, 128:256]).astype(bf16)
        gs_rr[q] = rows(part[56:64, 0:128], part[56:64, 128:256]).astype(bf16)
        return carry

    def back_part(n, k, src, dst, part, size):
        at = pl.ds(part * size, size)
        return Link(src.at[at], dst.at[at], gs_sem.at[n, part], gr_sem.at[n, part], k)

    back = [
        [
            back_part(2, 2, gs_rr, gr_ll, part, 4),
            back_part(3, -2, gs_ll, gr_rr, part, 4),
            back_part(0, 1, gs_r, gr_l, part, 8),
            back_part(1, -1, gs_l, gr_r, part, 8),
        ]
        for part in range(2)
    ]
    def half(step, part):
        lax.fori_loop(4 * part, 4 * part + 4, step, 0, unroll=4)

    half(back_step, 0)
    half(back_step, 1)
    half(low_step, 0)
    half(lift_step, 0)
    start_all(back[0])
    half(low_step, 1)
    half(lift_step, 1)
    start_all(back[1])

    for copy in sums:
        copy.wait_send()
    sent_all(halo[0] + halo[1] + back[0])
    for copy in sums:
        copy.wait_recv()
    tile = psend[...]
    for k in range(1, blk):
        tile = tile + pbuf[k]
    full = jnp.sum(tile, axis=1, keepdims=True)
    norm = jnp.sqrt(full / month_ref.size + 1e-05)
    scale = jnp.broadcast_to(step_size / norm, (8, 128))

    for q in range(8):
        if q % 4 == 0:
            got_all(back[q // 4])
        far_l = gr_ll[q].astype(f32)
        far_r = gr_rr[q].astype(f32)
        for i in range(2):
            l = 2 * q + i
            near = gr_l[l].astype(f32) + gr_r[l].astype(f32)
            far = (far_l[8 * i:8 * i + 8], far_r[8 * i:8 * i + 8])
            for m in range(2):
                g = grad[m, l] + near[8 * m:8 * m + 8] + far[m]
                out_ref[m, l] = base[m, l] - scale * g

    sent_all(back[1])


def shards(
    blk,
    sample, fresh_noise, proxy_month, proxy_cell, proxy_var, observed, proxy_weight,
    lift_weight, month_kernels, grid_kernels, read_weight,
):
    def grid(x):
        return x.reshape(32, 128)

    vmem = pltpu.VMEM
    dma = pltpu.SemaphoreType.DMA
    scratch = [
        vmem(sample.shape, f32), vmem(sample.shape, f32),
        vmem((32, 128), jnp.int32), vmem((32, 128), jnp.int32), vmem((32, 128), jnp.int32),
        vmem((32, 128), f32), vmem((32, 128), f32),
        vmem((8, 64), bf16), vmem(month_kernels.shape, bf16), vmem(grid_kernels.shape, bf16),
        vmem((8, 64), bf16),
        vmem((16, 16, 128), bf16), vmem((8, 16, 128), bf16), vmem((8, 16, 128), bf16),
        vmem((16, 16, 128), bf16), vmem((16, 16, 128), bf16),
        vmem((8, 16, 128), bf16), vmem((8, 16, 128), bf16),
        vmem((768, 256), bf16), vmem((64, 192), bf16),
        vmem((128, 768), bf16), vmem((128, 768), bf16), vmem((384, 256), bf16), vmem((384, 256), bf16),
        vmem((192, 64), bf16), vmem((128, 768), bf16),
        vmem((16, 128), bf16), vmem((128, 32), bf16),
        vmem((256, 512), f32),
        vmem((8, 32, 256), bf16),
        vmem((8, 384, 256), bf16), vmem((8, 128, 256), bf16), vmem((8, 768, 256), bf16),
        vmem((8, 384, 256), bf16), vmem((8, 2, 64, 256), bf16), vmem((8, 128, 256), bf16),
        vmem((8, 128, 256), bf16),
        vmem((3, 18, 64, 256), bf16), vmem((3, 18, 64, 256), bf16),
        vmem((18, 64, 256), bf16), vmem((18, 64, 256), bf16),
        vmem((8, 128, 256), f32), vmem((8, 128, 256), f32),
        vmem((2, 16, 8, 128), f32), vmem((2, 16, 8, 128), f32),
        vmem((16, 16, 128), bf16), vmem((16, 16, 128), bf16),
        vmem((8, 16, 128), bf16), vmem((8, 16, 128), bf16),
        vmem((16, 16, 128), bf16), vmem((16, 16, 128), bf16),
        vmem((8, 16, 128), bf16), vmem((8, 16, 128), bf16),
        vmem((1, 128), f32), vmem((blk, 1, 128), f32),
        dma((4, 4)), dma((4, 4)), dma((4, 4)), dma((4, 4)), dma((blk,)), dma((blk,)), dma((11,)),
        pltpu.SemaphoreType.REGULAR, pltpu.SemaphoreType.REGULAR, pltpu.SemaphoreType.REGULAR,
    ]
    return pl.pallas_call(
        functools.partial(kernel, blk),
        out_shape=jax.ShapeDtypeStruct(sample.shape, f32),
        in_specs=[pl.BlockSpec(memory_space=pl.ANY)] * 11,
        out_specs=pl.BlockSpec(memory_space=pltpu.VMEM),
        scratch_shapes=scratch,
        compiler_params=pltpu.CompilerParams(collective_id=0, has_side_effects=True, vmem_limit_bytes=32 * 1024 * 1024),
        name="guided_step",
    )(*[pltpu.with_memory_space_constraint(x, pltpu.HBM) for x in (
        sample, fresh_noise, grid(proxy_month), grid(proxy_cell), grid(proxy_var),
        grid(observed), grid(proxy_weight), lift_weight.T, month_kernels, grid_kernels, read_weight,
    )])


def solution(mesh):
    in_specs = (
        P(("win", "blk"), None, None, None),
        P(("win", "blk"), None, None, None),
        P("win"),
        P("win"),
        P("win"),
        P("win"),
        P("win"),
        P(),
        P(),
        P(),
        P(),
    )
    out_specs = P(("win", "blk"), None, None, None)
    return jax.shard_map(
        functools.partial(shards, mesh.shape["blk"]),
        mesh=mesh, in_specs=in_specs, out_specs=out_specs, check_vma=False,
    )
```

```python
import functools

import jax
import jax.numpy as jnp
from jax import lax
from jax.experimental import pallas as pl
from jax.experimental.pallas import tpu as pltpu
from jax.sharding import PartitionSpec as P

tweedie_gain = 0.5
step_size = 0.25
guide_gain = 4.0
noise_gain = 0.5**0.5

f32 = jnp.float32
bf16 = jnp.bfloat16
MESH = pl.DeviceIdType.MESH

gelu_c = 0.7978845608028654
gelu_ca = gelu_c * 0.044715


def gelu_parts(x):
    x2 = x * x
    u = x * (gelu_c + gelu_ca * x2)
    h = 0.5 * jnp.tanh(u) + 0.5
    g = x * h
    dg = h + (g - g * h) * (2.0 * gelu_c + 6.0 * gelu_ca * x2)
    return g, dg


def dot(a, b):
    return jnp.dot(a, b, preferred_element_type=f32)


def dot_nt(a, b):
    return lax.dot_general(a, b, (((1,), (1,)), ((), ())), preferred_element_type=f32)


def lanes(*parts):
    return jnp.concatenate(parts, axis=1)


def rows(*parts):
    return jnp.concatenate(parts, axis=0)


def grid_weights(block):
    zero = jnp.zeros((64, 64), f32)
    upper, lower = [], []
    for b in range(3):
        taps = [block(a, b) for a in range(3)]
        upper += taps + [zero]
        lower += [zero] + taps
    return rows(lanes(*upper), lanes(*lower)).astype(bf16)


def grid_weights_tall(block):
    zero = jnp.zeros((64, 64), f32)
    taps = []
    for b in range(3):
        k = [block(a, b) for a in range(3)]
        taps.append(rows(lanes(*k, zero), lanes(zero, *k)))
    return rows(*[taps[b][16 * g:16 * g + 16] for g in range(8) for b in range(3)]).astype(bf16)


def lon_sum(out, first, last):
    groups = []
    for g in range(8):
        halves = []
        for m in range(2):
            tap = [out[48 * g + 16 * b:48 * g + 16 * b + 16, 128 * m:128 * m + 128] for b in range(3)]
            left = jnp.where(first, 0.0, pltpu.roll(tap[0], 1, 1))
            right = jnp.where(last, 0.0, pltpu.roll(tap[2], 127, 1))
            halves.append(tap[1] + left + right)
        groups.append(lanes(*halves))
    return rows(*groups)


def kernel(
    blk,
    sample_in, noise_in, month_in, cell_in, var_in, obs_in, pw_in,
    lift_in, mk_in, gk_in, read_in,
    out_ref,
    sample_ref, noise_ref, month_ref, cell_ref, var_ref, obs_ref, pw_ref,
    lift_ref, mk_ref, gk_ref, read_ref,
    send_pair, send_lo, send_hi, halo_l, halo_r, halo_ll, halo_rr,
    wf1, wf2, wf3, wf4, wb4, wb3, wb2, wb1, wread, wreadt,
    field,
    f4s, h1s, h4s, a1s, g1, g2, g3, g4, h2s, h3s, s4s, s3s, a4, a3,
    base, grad,
    gs_l, gs_r, gs_ll, gs_rr, gr_l, gr_r, gr_ll, gr_rr,
    psend, pbuf,
    hs_sem, hr_sem, gs_sem, gr_sem, ps_sem, pr_sem, in_sem, near_sem, far_sem,
):
    me = lax.axis_index("blk")

    def peer(k):
        return lax.rem(me + k + blk, blk)

    def remote(src, dst, ssem, rsem, k):
        return pltpu.make_async_remote_copy(
            src_ref=src, dst_ref=dst, send_sem=ssem, recv_sem=rsem,
            device_id={"blk": peer(k)}, device_id_type=MESH,
        )

    def signal(sem, k):
        pl.semaphore_signal(sem, inc=1, device_id={"blk": peer(k)}, device_id_type=MESH)

    barrier = pltpu.get_barrier_semaphore()
    for k in (2, -2, 1, -1):
        signal(barrier, k)

    loads = [
        pltpu.make_async_copy(src, dst, in_sem.at[n])
        for n, (src, dst) in enumerate((
            (sample_in, sample_ref), (mk_in, mk_ref), (lift_in, lift_ref), (gk_in, gk_ref),
            (read_in, read_ref), (month_in, month_ref), (cell_in, cell_ref), (var_in, var_ref),
            (obs_in, obs_ref), (pw_in, pw_ref), (noise_in, noise_ref),
        ))
    ]
    for copy in loads:
        copy.start()
    loads[0].wait()

    for l in range(16):
        send_pair[l] = rows(sample_ref[0, l], sample_ref[1, l]).astype(bf16)
    for q in range(8):
        send_lo[q] = rows(sample_ref[0, 2 * q], sample_ref[0, 2 * q + 1]).astype(bf16)
        send_hi[q] = rows(sample_ref[1, 2 * q], sample_ref[1, 2 * q + 1]).astype(bf16)

    pl.semaphore_wait(barrier, 4)

    def halo_part(n, k, src, dst, part, size):
        at = pl.ds(part * size, size)
        return remote(src.at[at], dst.at[at], hs_sem.at[n, part], hr_sem.at[n, part], k)

    halo = [
        [
            halo_part(2, 2, send_hi, halo_ll, part, 4),
            halo_part(3, -2, send_lo, halo_rr, part, 4),
            halo_part(0, 1, send_pair, halo_l, part, 8),
            halo_part(1, -1, send_pair, halo_r, part, 8),
        ]
        for part in range(2)
    ]
    for part in halo:
        for copy in part:
            copy.start()
    for k in (2, -2):
        signal(near_sem, k)
    for copy in loads[1:10]:
        copy.wait()

    has_l = jnp.where(me > 0, 1.0, 0.0).astype(f32)
    has_ll = jnp.where(me > 1, 1.0, 0.0).astype(f32)
    has_r = jnp.where(me < blk - 1, 1.0, 0.0).astype(f32)
    has_rr = jnp.where(me < blk - 2, 1.0, 0.0).astype(f32)

    lift = lift_ref[...]
    pick = (lax.broadcasted_iota(jnp.int32, (8, 64), 1) % 8
            == lax.broadcasted_iota(jnp.int32, (8, 64), 0))
    pick = jnp.where(pick, 1.0, 0.0).astype(bf16)
    tiled = lax.dot_general(
        lift, pick, (((0,), (0,)), ((), ())), preferred_element_type=f32
    )
    col_month = lax.broadcasted_iota(jnp.int32, (64, 64), 1) // 8
    placed = [jnp.where(col_month == i, tiled, 0.0) for i in range(8)]
    placed_b = [x.astype(bf16) for x in placed]
    inner_rows = []
    for j in range(6):
        acc = dot(mk_ref[0, 0], placed_b[j])
        acc = acc + dot(mk_ref[0, 1], placed_b[j + 1])
        acc = acc + dot(mk_ref[0, 2], placed_b[j + 2])
        inner_rows.append(acc)
    both = rows(*[x for j in range(6) for x in (inner_rows[j], placed[j + 1])])
    both_hi = both.astype(bf16).astype(f32)
    both_lo = both - both_hi
    wf1[...] = lanes(both_hi, both_lo, both_hi, jnp.zeros_like(both)).astype(bf16)
    flipped_hi = jnp.transpose(both_hi)
    flipped_lo = jnp.transpose(both_lo)
    wb1[...] = rows(flipped_hi, flipped_lo).astype(bf16)

    def mk(k):
        return mk_ref[1, k].astype(f32)

    wf2[...] = lanes(mk(0) * has_l, mk(1), mk(2) * has_r).astype(bf16)
    wb2[...] = rows(
        jnp.transpose(mk(0)) * has_l, jnp.transpose(mk(1)), jnp.transpose(mk(2)) * has_r
    ).astype(bf16)
    wf3[...] = grid_weights(lambda a, b: gk_ref[0, a, b].astype(f32))
    wf4[...] = grid_weights(lambda a, b: gk_ref[1, a, b].astype(f32))
    wb3[...] = grid_weights_tall(lambda a, b: jnp.transpose(gk_ref[0, 2 - a, 2 - b].astype(f32)))
    wb4[...] = grid_weights_tall(lambda a, b: jnp.transpose(gk_ref[1, 2 - a, 2 - b].astype(f32)))
    read = read_ref[...].astype(f32)
    zero_read = jnp.zeros((8, 64), f32)
    wide = rows(lanes(read, zero_read), lanes(zero_read, read))
    wread[...] = wide.astype(bf16)
    tall = jnp.transpose(wide)
    wreadt[...] = lanes(tall, tall).astype(bf16)

    local = month_ref[...] - 2 * me
    owned = jnp.logical_and(local >= 0, local < 2)
    cell = cell_ref[...]
    row_of = jnp.where(owned, (local * 16 + lax.shift_right_logical(cell, 7)) * 8 + var_ref[...], -1)
    lon_of = jnp.bitwise_and(cell, 127)
    weight = pw_ref[...]
    weighted = weight * obs_ref[...]
    w_hi = weight.astype(bf16).astype(f32)
    w_lo = (weight - w_hi).astype(bf16).astype(f32)
    b_hi = weighted.astype(bf16).astype(f32)
    b_lo = (weighted - b_hi).astype(bf16).astype(f32)
    b_sum = b_hi + b_lo
    spread_terms = jnp.where(owned, b_sum * b_sum / (w_hi + w_lo), 0.0)
    within = (spread_terms[0:8] + spread_terms[8:16]) + (spread_terms[16:24] + spread_terms[24:32])
    row_iota = lax.broadcasted_iota(jnp.int32, (256, 128), 0)
    lon_iota = lax.broadcasted_iota(jnp.int32, (128, 128), 0)
    for c in range(4):
        lhs, rhs = [], []
        for r in range(8 * c, 8 * c + 8):
            lhs.append(jnp.where(row_iota == row_of[r:r + 1], 1.0, 0.0).astype(bf16))
            at = lon_iota == lon_of[r:r + 1]
            rhs.append(rows(*[
                jnp.where(at, x[r:r + 1], 0.0).astype(bf16) for x in (w_hi, w_lo, b_hi, b_lo)
            ]))
        part = dot_nt(lanes(*lhs), lanes(*rhs))
        if c == 0:
            field[...] = part
        else:
            field[...] += part
    w_field = field[:, 0:128] + field[:, 128:256]
    b_field = field[:, 256:384] + field[:, 384:512]
    mean = jnp.where(w_field > 0.0, b_field / jnp.where(w_field > 0.0, w_field, 1.0), 0.0)
    field[:, 0:128] = w_field
    field[:, 128:256] = mean
    taken = b_field * mean
    for r in range(32):
        within = within - taken[8 * r:8 * r + 8]

    zero_row = jnp.zeros((64, 256), bf16)
    for ref in (s4s, s3s):
        ref[0] = zero_row
        ref[17] = zero_row
    for ref in (h2s, h3s):
        for tap in range(3):
            ref[tap, 0] = zero_row
            ref[tap, 17] = zero_row

    lane = lax.broadcasted_iota(jnp.int32, (128, 128), 1)
    first, last = lane == 0, lane == 127
    lane16 = lax.broadcasted_iota(jnp.int32, (16, 128), 1)
    first16, last16 = lane16 == 0, lane16 == 127
    zero_half = jnp.zeros((128, 128), bf16)

    def window(ref, q):
        return rows(*[ref[tap, pl.ds(2 * q, 4)].reshape(256, 256) for tap in range(3)])

    def rows4(ref, q):
        return ref[pl.ds(2 * q, 4)].reshape(256, 256)

    def pair(ref, q):
        return ref[1, pl.ds(2 * q + 1, 2)].reshape(128, 256)

    def put(ref, q, value):
        left, right = [], []
        for m in range(2):
            half = value[:, 128 * m:128 * m + 128]
            left.append(jnp.where(first, zero_half, pltpu.roll(half, 1, 1)))
            right.append(jnp.where(last, zero_half, pltpu.roll(half, 127, 1)))
        at = pl.ds(2 * q + 1, 2)
        ref[0, at] = lanes(*left).reshape(2, 64, 256)
        ref[1, at] = value.reshape(2, 64, 256)
        ref[2, at] = lanes(*right).reshape(2, 64, 256)

    def month_step(q, carry):
        highs, lows = [], []
        for i in range(2):
            l = 2 * q + i
            prev = halo_l[l].astype(f32) * has_l
            nxt = halo_r[l].astype(f32) * has_r
            prev2 = halo_ll[q].astype(f32)[8 * i:8 * i + 8] * has_ll
            nxt2 = halo_rr[q].astype(f32)[8 * i:8 * i + 8] * has_rr
            own = rows(sample_ref[0, l], sample_ref[1, l])
            own_hi = own.astype(bf16).astype(f32)
            highs.append(rows(prev2, prev, own_hi, nxt, nxt2))
            z = jnp.zeros((24, 128), f32)
            lows.append(rows(z, own - own_hi, z))
        high = lanes(*highs)
        src = rows(high, high, lanes(*lows), jnp.zeros((64, 256), f32)).astype(bf16)
        out = dot(wf1[...], src).astype(bf16)
        hidden = []
        for j in range(6):
            gel, der = gelu_parts(out[128 * j:128 * j + 64])
            g1[q, 64 * j:64 * j + 64] = der
            hidden.append(out[128 * j + 64:128 * j + 128] + gel)
        h1s[q] = rows(*hidden)
        return carry

    def month_step2(q, carry):
        halves = []
        for m in range(2):
            src2 = rows(*[h1s[q, 64 * j:64 * j + 64] for j in (m, m + 2, m + 4)])
            gel2, der2 = gelu_parts(dot(wf2[...], src2).astype(bf16))
            g2[q, m] = der2
            nxt_h = h1s[q, 64 * (m + 2):64 * (m + 3)] + gel2
            halves.append(rows(nxt_h[:, 0:128], nxt_h[:, 128:256]))
        put(h2s, q, lanes(*halves))
        return carry


    def grid_step(q, carry):
        inner = dot(wf3[...], window(h2s, q)).astype(bf16)
        gel, der = gelu_parts(inner)
        g3[q] = der
        put(h3s, q, pair(h2s, q) + gel)
        return carry


    def last_step(q, carry):
        inner = dot(wf4[...], window(h3s, q)).astype(bf16)
        gel, der = gelu_parts(inner)
        g4[q] = der
        h4s[q] = pair(h3s, q) + gel
        return carry


    def top_step(q, total):
        score = dot(wread[...], h4s[q])
        forces = []
        for i in range(2):
            l = 2 * q + i
            line = []
            for m in range(2):
                sc = score[8 * i:8 * i + 8, 128 * m:128 * m + 128]
                sm = sample_ref[m, l]
                at = pl.ds((m * 16 + l) * 8, 8)
                w = field[at, 0:128]
                delta = sm + tweedie_gain * sc - field[at, 128:256]
                pull = w * delta
                total = total + pull * delta
                force = guide_gain * pull
                base[m, l] = sm + step_size * sc + noise_gain * noise_ref[m, l]
                grad[m, l] = force
                line.append(tweedie_gain * force)
            forces.append(lanes(*line))
        force = rows(*forces)
        force_hi = force.astype(bf16).astype(f32)
        f4s[q] = rows(force_hi, force - force_hi).astype(bf16)
        return total

    def adjoint_step(q, carry):
        adj = dot(wreadt[...], f4s[q])
        a4[q] = adj
        s4s[pl.ds(2 * q + 1, 2)] = (adj.astype(bf16) * g4[q]).reshape(2, 64, 256)
        return carry

    def run(step, part, carry=0):
        return lax.fori_loop(2 * part, 2 * part + 2, step, carry, unroll=2)

    pl.semaphore_wait(near_sem, 2)
    for k in (4, -4):
        signal(far_sem, k)
    loads[10].wait()
    total = within
    for part in range(2):
        for copy in halo[part]:
            copy.wait_recv()
        lax.fori_loop(4 * part, 4 * part + 4, month_step, 0, unroll=4)
    lax.fori_loop(0, 8, month_step2, 0, unroll=8)
    lax.fori_loop(0, 8, grid_step, 0, unroll=8)
    lax.fori_loop(0, 8, last_step, 0, unroll=8)
    total = lax.fori_loop(0, 8, top_step, total, unroll=8)

    psend[...] = jnp.sum(total, axis=0, keepdims=True)
    pl.semaphore_wait(far_sem, 2)
    sums = [
        remote(psend, pbuf.at[k], ps_sem.at[k], pr_sem.at[k], k) for k in range(1, blk)
    ]
    for copy in sums:
        copy.start()
    lax.fori_loop(0, 8, adjoint_step, 0, unroll=8)

    def back_step(q, carry):
        adj = a4[q] + lon_sum(dot(wb4[...], rows4(s4s, q)), first16, last16)
        a3[q] = adj
        s3s[pl.ds(2 * q + 1, 2)] = (adj.astype(bf16) * g3[q]).reshape(2, 64, 256)
        return carry


    def low_step(q, carry):
        adj2 = a3[q] + lon_sum(dot(wb3[...], rows4(s3s, q)), first16, last16)
        own, pushed = [], []
        for m in range(2):
            cols = slice(128 * m, 128 * m + 128)
            adj = lanes(adj2[0:64, cols], adj2[64:128, cols])
            own.append(adj)
            scaled = adj.astype(bf16) * g2[q, m]
            pushed.append(dot(wb2[...], scaled))
        adj1 = [
            pushed[0][0:64], pushed[1][0:64],
            own[0] + pushed[0][64:128], own[1] + pushed[1][64:128],
            pushed[0][128:192], pushed[1][128:192],
        ]
        src = []
        for j in range(6):
            adj = adj1[j].astype(bf16)
            src += [adj * g1[q, 64 * j:64 * j + 64], adj]
        a1s[q] = rows(*src)
        return carry


    def lift_step(q, carry):
        both = dot(wb1[...], a1s[q])
        part = both[0:64] + both[64:128]
        for i in range(2):
            l = 2 * q + i
            cols = slice(128 * i, 128 * i + 128)
            gs_l[l] = part[8:24, cols].astype(bf16)
            gs_r[l] = part[40:56, cols].astype(bf16)
            for m in range(2):
                grad[m, l] += part[24 + 8 * m:32 + 8 * m, cols]
        gs_ll[q] = rows(part[0:8, 0:128], part[0:8, 128:256]).astype(bf16)
        gs_rr[q] = rows(part[56:64, 0:128], part[56:64, 128:256]).astype(bf16)
        return carry

    def back_part(n, k, src, dst, part, size):
        at = pl.ds(part * size, size)
        return remote(src.at[at], dst.at[at], gs_sem.at[n, part], gr_sem.at[n, part], k)

    back = [
        [
            back_part(2, 2, gs_rr, gr_ll, part, 4),
            back_part(3, -2, gs_ll, gr_rr, part, 4),
            back_part(0, 1, gs_r, gr_l, part, 8),
            back_part(1, -1, gs_l, gr_r, part, 8),
        ]
        for part in range(2)
    ]
    def half(step, part):
        lax.fori_loop(4 * part, 4 * part + 4, step, 0, unroll=4)

    half(back_step, 0)
    half(back_step, 1)
    half(low_step, 0)
    half(lift_step, 0)
    for copy in back[0]:
        copy.start()
    half(low_step, 1)
    half(lift_step, 1)
    for copy in back[1]:
        copy.start()

    for copy in sum(halo, sums) + sum(back[:1], []):
        copy.wait_send()
    for copy in sums:
        copy.wait_recv()
    tile = psend[...]
    for k in range(1, blk):
        tile = tile + pbuf[k]
    full = jnp.sum(tile, axis=1, keepdims=True)
    norm = jnp.sqrt(full / month_ref.size + 1e-05)
    scale = jnp.broadcast_to(step_size / norm, (8, 128))

    for q in range(8):
        if q % 4 == 0:
            for copy in back[q // 4]:
                copy.wait_recv()
        far_l = gr_ll[q].astype(f32) * has_ll
        far_r = gr_rr[q].astype(f32) * has_rr
        for i in range(2):
            l = 2 * q + i
            near = gr_l[l].astype(f32) * has_l + gr_r[l].astype(f32) * has_r
            far = (far_l[8 * i:8 * i + 8], far_r[8 * i:8 * i + 8])
            for m in range(2):
                g = grad[m, l] + near[8 * m:8 * m + 8] + far[m]
                out_ref[m, l] = base[m, l] - scale * g

    for copy in back[1]:
        copy.wait_send()


def shards(
    blk,
    sample, fresh_noise, proxy_month, proxy_cell, proxy_var, observed, proxy_weight,
    lift_weight, month_kernels, grid_kernels, read_weight,
):
    def grid(x):
        return x.reshape(32, 128)

    vmem = pltpu.VMEM
    dma = pltpu.SemaphoreType.DMA
    scratch = [
        vmem(sample.shape, f32), vmem(sample.shape, f32),
        vmem((32, 128), jnp.int32), vmem((32, 128), jnp.int32), vmem((32, 128), jnp.int32),
        vmem((32, 128), f32), vmem((32, 128), f32),
        vmem((8, 64), bf16), vmem(month_kernels.shape, bf16), vmem(grid_kernels.shape, bf16),
        vmem((8, 64), bf16),
        vmem((16, 16, 128), bf16), vmem((8, 16, 128), bf16), vmem((8, 16, 128), bf16),
        vmem((16, 16, 128), bf16), vmem((16, 16, 128), bf16),
        vmem((8, 16, 128), bf16), vmem((8, 16, 128), bf16),
        vmem((768, 256), bf16), vmem((64, 192), bf16),
        vmem((128, 768), bf16), vmem((128, 768), bf16), vmem((384, 256), bf16), vmem((384, 256), bf16),
        vmem((192, 64), bf16), vmem((128, 768), bf16),
        vmem((16, 128), bf16), vmem((128, 32), bf16),
        vmem((256, 512), f32),
        vmem((8, 32, 256), bf16),
        vmem((8, 384, 256), bf16), vmem((8, 128, 256), bf16), vmem((8, 768, 256), bf16),
        vmem((8, 384, 256), bf16), vmem((8, 2, 64, 256), bf16), vmem((8, 128, 256), bf16),
        vmem((8, 128, 256), bf16),
        vmem((3, 18, 64, 256), bf16), vmem((3, 18, 64, 256), bf16),
        vmem((18, 64, 256), bf16), vmem((18, 64, 256), bf16),
        vmem((8, 128, 256), f32), vmem((8, 128, 256), f32),
        vmem((2, 16, 8, 128), f32), vmem((2, 16, 8, 128), f32),
        vmem((16, 16, 128), bf16), vmem((16, 16, 128), bf16),
        vmem((8, 16, 128), bf16), vmem((8, 16, 128), bf16),
        vmem((16, 16, 128), bf16), vmem((16, 16, 128), bf16),
        vmem((8, 16, 128), bf16), vmem((8, 16, 128), bf16),
        vmem((1, 128), f32), vmem((blk, 1, 128), f32),
        dma((4, 4)), dma((4, 4)), dma((4, 4)), dma((4, 4)), dma((blk,)), dma((blk,)), dma((11,)),
        pltpu.SemaphoreType.REGULAR, pltpu.SemaphoreType.REGULAR,
    ]
    return pl.pallas_call(
        functools.partial(kernel, blk),
        out_shape=jax.ShapeDtypeStruct(sample.shape, f32),
        in_specs=[pl.BlockSpec(memory_space=pl.ANY)] * 11,
        out_specs=pl.BlockSpec(memory_space=pltpu.VMEM),
        scratch_shapes=scratch,
        compiler_params=pltpu.CompilerParams(collective_id=0, has_side_effects=True, vmem_limit_bytes=32 * 1024 * 1024),
        name="guided_step",
    )(*[pltpu.with_memory_space_constraint(x, pltpu.HBM) for x in (
        sample, fresh_noise, grid(proxy_month), grid(proxy_cell), grid(proxy_var),
        grid(observed), grid(proxy_weight), lift_weight.T, month_kernels, grid_kernels, read_weight,
    )])


def solution(mesh):
    in_specs = (
        P(("win", "blk"), None, None, None),
        P(("win", "blk"), None, None, None),
        P("win"),
        P("win"),
        P("win"),
        P("win"),
        P("win"),
        P(),
        P(),
        P(),
        P(),
    )
    out_specs = P(("win", "blk"), None, None, None)
    return jax.shard_map(
        functools.partial(shards, mesh.shape["blk"]),
        mesh=mesh, in_specs=in_specs, out_specs=out_specs, check_vma=False,
    )
```

```python
import functools

import jax
import jax.numpy as jnp
from jax import lax
from jax.experimental import pallas as pl
from jax.experimental.pallas import tpu as pltpu
from jax.sharding import PartitionSpec as P

tweedie_gain = 0.5
step_size = 0.25
guide_gain = 4.0
noise_gain = 0.5**0.5

f32 = jnp.float32
bf16 = jnp.bfloat16
MESH = pl.DeviceIdType.MESH

gelu_c = 0.7978845608028654
gelu_ca = gelu_c * 0.044715


def gelu_parts(x):
    x2 = x * x
    u = x * (gelu_c + gelu_ca * x2)
    h = 0.5 * jnp.tanh(u) + 0.5
    g = x * h
    dg = h + (g - g * h) * (2.0 * gelu_c + 6.0 * gelu_ca * x2)
    return g, dg


def dot(a, b):
    return jnp.dot(a, b, preferred_element_type=f32)


def dot_nt(a, b):
    return lax.dot_general(a, b, (((1,), (1,)), ((), ())), preferred_element_type=f32)


def lanes(*parts):
    return jnp.concatenate(parts, axis=1)


def rows(*parts):
    return jnp.concatenate(parts, axis=0)


def grid_weights(block):
    zero = jnp.zeros((64, 64), f32)
    upper, lower = [], []
    for b in range(3):
        taps = [block(a, b) for a in range(3)]
        upper += taps + [zero]
        lower += [zero] + taps
    return rows(lanes(*upper), lanes(*lower)).astype(bf16)


def grid_weights_tall(block):
    zero = jnp.zeros((64, 64), f32)
    taps = []
    for b in range(3):
        k = [block(a, b) for a in range(3)]
        taps.append(rows(lanes(*k, zero), lanes(zero, *k)))
    return rows(*[taps[b][16 * g:16 * g + 16] for g in range(8) for b in range(3)]).astype(bf16)


def lon_sum(out, first, last):
    groups = []
    for g in range(8):
        halves = []
        for m in range(2):
            tap = [out[48 * g + 16 * b:48 * g + 16 * b + 16, 128 * m:128 * m + 128] for b in range(3)]
            left = jnp.where(first, 0.0, pltpu.roll(tap[0], 1, 1))
            right = jnp.where(last, 0.0, pltpu.roll(tap[2], 127, 1))
            halves.append(tap[1] + left + right)
        groups.append(lanes(*halves))
    return rows(*groups)


def kernel(
    blk,
    sample_in, noise_in, month_in, cell_in, var_in, obs_in, pw_in,
    lift_in, mk_in, gk_in, read_in,
    out_ref,
    sample_ref, noise_ref, month_ref, cell_ref, var_ref, obs_ref, pw_ref,
    lift_ref, mk_ref, gk_ref, read_ref,
    send_pair, send_lo, send_hi, halo_l, halo_r, halo_ll, halo_rr,
    wf1, wf2, wf3, wf4, wb4, wb3, wb2, wb1, wread, wreadt,
    field,
    f4s, h1s, h4s, a1s, g1, g2, g3, g4, h2s, h3s, s4s, s3s, a4, a3,
    base, grad,
    gs_l, gs_r, gs_ll, gs_rr, gr_l, gr_r, gr_ll, gr_rr,
    psend, pbuf,
    hs_sem, hr_sem, gs_sem, gr_sem, ps_sem, pr_sem, in_sem, near_sem, far_sem, wide_sem,
):
    me = lax.axis_index("blk")

    def peer(k):
        return lax.rem(me + k + blk, blk)

    def remote(src, dst, ssem, rsem, k):
        return pltpu.make_async_remote_copy(
            src_ref=src, dst_ref=dst, send_sem=ssem, recv_sem=rsem,
            device_id={"blk": peer(k)}, device_id_type=MESH,
        )

    def there(k):
        return jnp.logical_and(me + k >= 0, me + k < blk)

    def count(*ks):
        return sum(jnp.where(there(k), 1, 0) for k in ks)

    def signal(sem, k):
        @pl.when(there(k))
        def _():
            pl.semaphore_signal(sem, inc=1, device_id={"blk": peer(k)}, device_id_type=MESH)

    class Link:
        def __init__(self, src, dst, ssem, rsem, k):
            self.copy, self.k = remote(src, dst, ssem, rsem, k), k

        def start(self):
            self.copy.start()

        def wait_send(self):
            self.copy.wait_send()

        def wait_recv(self):
            self.copy.wait_recv()

    inside = jnp.logical_and(me >= 2, me < blk - 2)

    def each(links, act, way):
        @pl.when(inside)
        def _():
            for link in links:
                act(link)

        @pl.when(jnp.logical_not(inside))
        def _():
            for link in links:
                pl.when(there(way * link.k))(functools.partial(act, link))

    def start_all(links):
        each(links, Link.start, 1)

    def sent_all(links):
        each(links, Link.wait_send, 1)

    def got_all(links):
        each(links, Link.wait_recv, -1)

    barrier = pltpu.get_barrier_semaphore()
    for k in (2, -2, 1, -1):
        signal(barrier, k)

    loads = [
        pltpu.make_async_copy(src, dst, in_sem.at[n])
        for n, (src, dst) in enumerate((
            (sample_in, sample_ref), (mk_in, mk_ref), (lift_in, lift_ref), (gk_in, gk_ref),
            (read_in, read_ref), (month_in, month_ref), (cell_in, cell_ref), (var_in, var_ref),
            (obs_in, obs_ref), (pw_in, pw_ref), (noise_in, noise_ref),
        ))
    ]
    for copy in loads:
        copy.start()
    loads[0].wait()

    for l in range(16):
        send_pair[l] = rows(sample_ref[0, l], sample_ref[1, l]).astype(bf16)
    for q in range(8):
        send_lo[q] = rows(sample_ref[0, 2 * q], sample_ref[0, 2 * q + 1]).astype(bf16)
        send_hi[q] = rows(sample_ref[1, 2 * q], sample_ref[1, 2 * q + 1]).astype(bf16)

    pl.semaphore_wait(barrier, count(1, -1, 2, -2))

    def halo_part(n, k, src, dst, part, size):
        at = pl.ds(part * size, size)
        return Link(src.at[at], dst.at[at], hs_sem.at[n, part], hr_sem.at[n, part], k)

    halo = [
        [
            halo_part(2, 2, send_hi, halo_ll, part, 4),
            halo_part(3, -2, send_lo, halo_rr, part, 4),
            halo_part(0, 1, send_pair, halo_l, part, 8),
            halo_part(1, -1, send_pair, halo_r, part, 8),
        ]
        for part in range(2)
    ]
    for part in halo:
        start_all(part)
    for k, bufs in ((-1, (halo_l, gr_l)), (1, (halo_r, gr_r)), (-2, (halo_ll, gr_ll)), (2, (halo_rr, gr_rr))):
        @pl.when(jnp.logical_not(there(k)))
        def _():
            for ref in bufs:
                ref[...] = jnp.zeros(ref.shape, bf16)
    for k in (2, -2):
        signal(near_sem, k)
    for copy in loads[1:10]:
        copy.wait()

    has_l = jnp.where(me > 0, 1.0, 0.0).astype(f32)
    has_r = jnp.where(me < blk - 1, 1.0, 0.0).astype(f32)

    lift = lift_ref[...]
    pick = (lax.broadcasted_iota(jnp.int32, (8, 64), 1) % 8
            == lax.broadcasted_iota(jnp.int32, (8, 64), 0))
    pick = jnp.where(pick, 1.0, 0.0).astype(bf16)
    tiled = lax.dot_general(
        lift, pick, (((0,), (0,)), ((), ())), preferred_element_type=f32
    )
    col_month = lax.broadcasted_iota(jnp.int32, (64, 64), 1) // 8
    placed = [jnp.where(col_month == i, tiled, 0.0) for i in range(8)]
    placed_b = [x.astype(bf16) for x in placed]
    inner_rows = []
    for j in range(6):
        acc = dot(mk_ref[0, 0], placed_b[j])
        acc = acc + dot(mk_ref[0, 1], placed_b[j + 1])
        acc = acc + dot(mk_ref[0, 2], placed_b[j + 2])
        inner_rows.append(acc)
    both = rows(*[x for j in range(6) for x in (inner_rows[j], placed[j + 1])])
    both_hi = both.astype(bf16).astype(f32)
    both_lo = both - both_hi
    wf1[...] = lanes(both_hi, both_lo, both_hi).astype(bf16)
    flipped_hi = jnp.transpose(both_hi)
    flipped_lo = jnp.transpose(both_lo)
    wb1[...] = rows(flipped_hi, flipped_lo).astype(bf16)

    def mk(k):
        return mk_ref[1, k].astype(f32)

    wf2[...] = lanes(mk(0) * has_l, mk(1), mk(2) * has_r).astype(bf16)
    wb2[...] = rows(
        jnp.transpose(mk(0)) * has_l, jnp.transpose(mk(1)), jnp.transpose(mk(2)) * has_r
    ).astype(bf16)
    wf3[...] = grid_weights(lambda a, b: gk_ref[0, a, b].astype(f32))
    wf4[...] = grid_weights(lambda a, b: gk_ref[1, a, b].astype(f32))
    wb3[...] = grid_weights_tall(lambda a, b: jnp.transpose(gk_ref[0, 2 - a, 2 - b].astype(f32)))
    wb4[...] = grid_weights_tall(lambda a, b: jnp.transpose(gk_ref[1, 2 - a, 2 - b].astype(f32)))
    read = read_ref[...].astype(f32)
    zero_read = jnp.zeros((8, 64), f32)
    wide = rows(lanes(read, zero_read), lanes(zero_read, read))
    wread[...] = wide.astype(bf16)
    tall = jnp.transpose(wide)
    wreadt[...] = lanes(tall, tall).astype(bf16)

    local = month_ref[...] - 2 * me
    owned = jnp.logical_and(local >= 0, local < 2)
    cell = cell_ref[...]
    row_of = jnp.where(owned, (local * 16 + lax.shift_right_logical(cell, 7)) * 8 + var_ref[...], -1)
    lon_of = jnp.bitwise_and(cell, 127)
    weight = pw_ref[...]
    weighted = weight * obs_ref[...]
    w_hi = weight.astype(bf16).astype(f32)
    w_lo = (weight - w_hi).astype(bf16).astype(f32)
    b_hi = weighted.astype(bf16).astype(f32)
    b_lo = (weighted - b_hi).astype(bf16).astype(f32)
    b_sum = b_hi + b_lo
    spread_terms = jnp.where(owned, b_sum * b_sum / (w_hi + w_lo), 0.0)
    within = (spread_terms[0:8] + spread_terms[8:16]) + (spread_terms[16:24] + spread_terms[24:32])
    row_iota = lax.broadcasted_iota(jnp.int32, (256, 128), 0)
    lon_iota = lax.broadcasted_iota(jnp.int32, (128, 128), 0)
    for c in range(4):
        lhs, rhs = [], []
        for r in range(8 * c, 8 * c + 8):
            lhs.append(jnp.where(row_iota == row_of[r:r + 1], 1.0, 0.0).astype(bf16))
            at = lon_iota == lon_of[r:r + 1]
            rhs.append(rows(*[
                jnp.where(at, x[r:r + 1], 0.0).astype(bf16) for x in (w_hi, w_lo, b_hi, b_lo)
            ]))
        part = dot_nt(lanes(*lhs), lanes(*rhs))
        if c == 0:
            field[...] = part
        else:
            field[...] += part
    w_field = field[:, 0:128] + field[:, 128:256]
    b_field = field[:, 256:384] + field[:, 384:512]
    mean = jnp.where(w_field > 0.0, b_field / jnp.where(w_field > 0.0, w_field, 1.0), 0.0)
    field[:, 0:128] = w_field
    field[:, 128:256] = mean
    taken = b_field * mean
    for r in range(32):
        within = within - taken[8 * r:8 * r + 8]

    zero_row = jnp.zeros((64, 256), bf16)
    for ref in (s4s, s3s):
        ref[0] = zero_row
        ref[17] = zero_row
    for ref in (h2s, h3s):
        for tap in range(3):
            ref[tap, 0] = zero_row
            ref[tap, 17] = zero_row

    lane = lax.broadcasted_iota(jnp.int32, (128, 128), 1)
    first, last = lane == 0, lane == 127
    lane16 = lax.broadcasted_iota(jnp.int32, (16, 128), 1)
    first16, last16 = lane16 == 0, lane16 == 127
    zero_half = jnp.zeros((128, 128), bf16)

    def window(ref, q):
        return rows(*[ref[tap, pl.ds(2 * q, 4)].reshape(256, 256) for tap in range(3)])

    def rows4(ref, q):
        return ref[pl.ds(2 * q, 4)].reshape(256, 256)

    def pair(ref, q):
        return ref[1, pl.ds(2 * q + 1, 2)].reshape(128, 256)

    def put(ref, q, value):
        left, right = [], []
        for m in range(2):
            half = value[:, 128 * m:128 * m + 128]
            left.append(jnp.where(first, zero_half, pltpu.roll(half, 1, 1)))
            right.append(jnp.where(last, zero_half, pltpu.roll(half, 127, 1)))
        at = pl.ds(2 * q + 1, 2)
        ref[0, at] = lanes(*left).reshape(2, 64, 256)
        ref[1, at] = value.reshape(2, 64, 256)
        ref[2, at] = lanes(*right).reshape(2, 64, 256)

    def month_step(q, carry):
        highs, lows = [], []
        for i in range(2):
            l = 2 * q + i
            prev = halo_l[l].astype(f32)
            nxt = halo_r[l].astype(f32)
            prev2 = halo_ll[q].astype(f32)[8 * i:8 * i + 8]
            nxt2 = halo_rr[q].astype(f32)[8 * i:8 * i + 8]
            own = rows(sample_ref[0, l], sample_ref[1, l])
            own_hi = own.astype(bf16).astype(f32)
            highs.append(rows(prev2, prev, own_hi, nxt, nxt2))
            z = jnp.zeros((24, 128), f32)
            lows.append(rows(z, own - own_hi, z))
        high = lanes(*highs)
        src = rows(high, high, lanes(*lows)).astype(bf16)
        out = dot(wf1[...], src).astype(bf16)
        hidden = []
        for j in range(6):
            gel, der = gelu_parts(out[128 * j:128 * j + 64])
            g1[q, 64 * j:64 * j + 64] = der
            hidden.append(out[128 * j + 64:128 * j + 128] + gel)
        h1s[q] = rows(*hidden)
        return carry

    def month_step2(q, carry):
        halves = []
        for m in range(2):
            src2 = rows(*[h1s[q, 64 * j:64 * j + 64] for j in (m, m + 2, m + 4)])
            gel2, der2 = gelu_parts(dot(wf2[...], src2).astype(bf16))
            g2[q, m] = der2
            nxt_h = h1s[q, 64 * (m + 2):64 * (m + 3)] + gel2
            halves.append(rows(nxt_h[:, 0:128], nxt_h[:, 128:256]))
        put(h2s, q, lanes(*halves))
        return carry


    def grid_step(q, carry):
        inner = dot(wf3[...], window(h2s, q)).astype(bf16)
        gel, der = gelu_parts(inner)
        g3[q] = der
        put(h3s, q, pair(h2s, q) + gel)
        return carry


    def last_step(q, carry):
        inner = dot(wf4[...], window(h3s, q)).astype(bf16)
        gel, der = gelu_parts(inner)
        g4[q] = der
        h4s[q] = pair(h3s, q) + gel
        return carry


    def top_step(q, total):
        score = dot(wread[...], h4s[q])
        forces = []
        for i in range(2):
            l = 2 * q + i
            line = []
            for m in range(2):
                sc = score[8 * i:8 * i + 8, 128 * m:128 * m + 128]
                sm = sample_ref[m, l]
                at = pl.ds((m * 16 + l) * 8, 8)
                w = field[at, 0:128]
                delta = sm + tweedie_gain * sc - field[at, 128:256]
                pull = w * delta
                total = total + pull * delta
                force = guide_gain * pull
                base[m, l] = sm + step_size * sc + noise_gain * noise_ref[m, l]
                grad[m, l] = force
                line.append(tweedie_gain * force)
            forces.append(lanes(*line))
        force = rows(*forces)
        force_hi = force.astype(bf16).astype(f32)
        f4s[q] = rows(force_hi, force - force_hi).astype(bf16)
        return total

    def adjoint_step(q, carry):
        adj = dot(wreadt[...], f4s[q])
        a4[q] = adj
        s4s[pl.ds(2 * q + 1, 2)] = (adj.astype(bf16) * g4[q]).reshape(2, 64, 256)
        return carry

    def run(step, part, carry=0):
        return lax.fori_loop(2 * part, 2 * part + 2, step, carry, unroll=2)

    pl.semaphore_wait(near_sem, count(2, -2))
    for k in (4, -4):
        signal(far_sem, k)
    loads[10].wait()
    total = within
    for part in range(2):
        got_all(halo[part])
        lax.fori_loop(4 * part, 4 * part + 4, month_step, 0, unroll=4)
    pl.semaphore_wait(far_sem, count(4, -4))
    for k in (8, -8):
        signal(wide_sem, k)
    lax.fori_loop(0, 8, month_step2, 0, unroll=8)
    lax.fori_loop(0, 8, grid_step, 0, unroll=8)
    lax.fori_loop(0, 8, last_step, 0, unroll=8)
    total = lax.fori_loop(0, 8, top_step, total, unroll=8)

    psend[...] = jnp.sum(total, axis=0, keepdims=True)
    pl.semaphore_wait(wide_sem, count(8, -8))
    sums = [
        remote(psend, pbuf.at[k], ps_sem.at[k], pr_sem.at[k], k) for k in range(1, blk)
    ]
    for copy in sums:
        copy.start()
    lax.fori_loop(0, 8, adjoint_step, 0, unroll=8)

    def back_step(q, carry):
        adj = a4[q] + lon_sum(dot(wb4[...], rows4(s4s, q)), first16, last16)
        a3[q] = adj
        s3s[pl.ds(2 * q + 1, 2)] = (adj.astype(bf16) * g3[q]).reshape(2, 64, 256)
        return carry


    def low_step(q, carry):
        adj2 = a3[q] + lon_sum(dot(wb3[...], rows4(s3s, q)), first16, last16)
        own, pushed = [], []
        for m in range(2):
            cols = slice(128 * m, 128 * m + 128)
            adj = lanes(adj2[0:64, cols], adj2[64:128, cols])
            own.append(adj)
            scaled = adj.astype(bf16) * g2[q, m]
            pushed.append(dot(wb2[...], scaled))
        adj1 = [
            pushed[0][0:64], pushed[1][0:64],
            own[0] + pushed[0][64:128], own[1] + pushed[1][64:128],
            pushed[0][128:192], pushed[1][128:192],
        ]
        src = []
        for j in range(6):
            adj = adj1[j].astype(bf16)
            src += [adj * g1[q, 64 * j:64 * j + 64], adj]
        a1s[q] = rows(*src)
        return carry


    def lift_step(q, carry):
        both = dot(wb1[...], a1s[q])
        part = both[0:64] + both[64:128]
        for i in range(2):
            l = 2 * q + i
            cols = slice(128 * i, 128 * i + 128)
            gs_l[l] = part[8:24, cols].astype(bf16)
            gs_r[l] = part[40:56, cols].astype(bf16)
            for m in range(2):
                grad[m, l] += part[24 + 8 * m:32 + 8 * m, cols]
        gs_ll[q] = rows(part[0:8, 0:128], part[0:8, 128:256]).astype(bf16)
        gs_rr[q] = rows(part[56:64, 0:128], part[56:64, 128:256]).astype(bf16)
        return carry

    def back_part(n, k, src, dst, part, size):
        at = pl.ds(part * size, size)
        return Link(src.at[at], dst.at[at], gs_sem.at[n, part], gr_sem.at[n, part], k)

    back = [
        [
            back_part(2, 2, gs_rr, gr_ll, part, 4),
            back_part(3, -2, gs_ll, gr_rr, part, 4),
            back_part(0, 1, gs_r, gr_l, part, 8),
            back_part(1, -1, gs_l, gr_r, part, 8),
        ]
        for part in range(2)
    ]
    def half(step, part):
        lax.fori_loop(4 * part, 4 * part + 4, step, 0, unroll=4)

    half(back_step, 0)
    half(back_step, 1)
    half(low_step, 0)
    half(lift_step, 0)
    start_all(back[0])
    half(low_step, 1)
    half(lift_step, 1)
    start_all(back[1])

    for copy in sums:
        copy.wait_send()
    sent_all(halo[0] + halo[1] + back[0])
    for copy in sums:
        copy.wait_recv()
    tile = psend[...]
    for k in range(1, blk):
        tile = tile + pbuf[k]
    full = jnp.sum(tile, axis=1, keepdims=True)
    norm = jnp.sqrt(full / month_ref.size + 1e-05)
    scale = jnp.broadcast_to(step_size / norm, (8, 128))

    for q in range(8):
        if q % 4 == 0:
            got_all(back[q // 4])
        far_l = gr_ll[q].astype(f32)
        far_r = gr_rr[q].astype(f32)
        for i in range(2):
            l = 2 * q + i
            near = gr_l[l].astype(f32) + gr_r[l].astype(f32)
            far = (far_l[8 * i:8 * i + 8], far_r[8 * i:8 * i + 8])
            for m in range(2):
                g = grad[m, l] + near[8 * m:8 * m + 8] + far[m]
                out_ref[m, l] = base[m, l] - scale * g

    sent_all(back[1])


def shards(
    blk,
    sample, fresh_noise, proxy_month, proxy_cell, proxy_var, observed, proxy_weight,
    lift_weight, month_kernels, grid_kernels, read_weight,
):
    def grid(x):
        return x.reshape(32, 128)

    vmem = pltpu.VMEM
    dma = pltpu.SemaphoreType.DMA
    scratch = [
        vmem(sample.shape, f32), vmem(sample.shape, f32),
        vmem((32, 128), jnp.int32), vmem((32, 128), jnp.int32), vmem((32, 128), jnp.int32),
        vmem((32, 128), f32), vmem((32, 128), f32),
        vmem((8, 64), bf16), vmem(month_kernels.shape, bf16), vmem(grid_kernels.shape, bf16),
        vmem((8, 64), bf16),
        vmem((16, 16, 128), bf16), vmem((8, 16, 128), bf16), vmem((8, 16, 128), bf16),
        vmem((16, 16, 128), bf16), vmem((16, 16, 128), bf16),
        vmem((8, 16, 128), bf16), vmem((8, 16, 128), bf16),
        vmem((768, 192), bf16), vmem((64, 192), bf16),
        vmem((128, 768), bf16), vmem((128, 768), bf16), vmem((384, 256), bf16), vmem((384, 256), bf16),
        vmem((192, 64), bf16), vmem((128, 768), bf16),
        vmem((16, 128), bf16), vmem((128, 32), bf16),
        vmem((256, 512), f32),
        vmem((8, 32, 256), bf16),
        vmem((8, 384, 256), bf16), vmem((8, 128, 256), bf16), vmem((8, 768, 256), bf16),
        vmem((8, 384, 256), bf16), vmem((8, 2, 64, 256), bf16), vmem((8, 128, 256), bf16),
        vmem((8, 128, 256), bf16),
        vmem((3, 18, 64, 256), bf16), vmem((3, 18, 64, 256), bf16),
        vmem((18, 64, 256), bf16), vmem((18, 64, 256), bf16),
        vmem((8, 128, 256), f32), vmem((8, 128, 256), f32),
        vmem((2, 16, 8, 128), f32), vmem((2, 16, 8, 128), f32),
        vmem((16, 16, 128), bf16), vmem((16, 16, 128), bf16),
        vmem((8, 16, 128), bf16), vmem((8, 16, 128), bf16),
        vmem((16, 16, 128), bf16), vmem((16, 16, 128), bf16),
        vmem((8, 16, 128), bf16), vmem((8, 16, 128), bf16),
        vmem((1, 128), f32), vmem((blk, 1, 128), f32),
        dma((4, 4)), dma((4, 4)), dma((4, 4)), dma((4, 4)), dma((blk,)), dma((blk,)), dma((11,)),
        pltpu.SemaphoreType.REGULAR, pltpu.SemaphoreType.REGULAR, pltpu.SemaphoreType.REGULAR,
    ]
    return pl.pallas_call(
        functools.partial(kernel, blk),
        out_shape=jax.ShapeDtypeStruct(sample.shape, f32),
        in_specs=[pl.BlockSpec(memory_space=pl.ANY)] * 11,
        out_specs=pl.BlockSpec(memory_space=pltpu.VMEM),
        scratch_shapes=scratch,
        compiler_params=pltpu.CompilerParams(collective_id=0, has_side_effects=True, vmem_limit_bytes=32 * 1024 * 1024),
        name="guided_step",
    )(*[pltpu.with_memory_space_constraint(x, pltpu.HBM) for x in (
        sample, fresh_noise, grid(proxy_month), grid(proxy_cell), grid(proxy_var),
        grid(observed), grid(proxy_weight), lift_weight.T, month_kernels, grid_kernels, read_weight,
    )])


def solution(mesh):
    in_specs = (
        P(("win", "blk"), None, None, None),
        P(("win", "blk"), None, None, None),
        P("win"),
        P("win"),
        P("win"),
        P("win"),
        P("win"),
        P(),
        P(),
        P(),
        P(),
    )
    out_specs = P(("win", "blk"), None, None, None)
    return jax.shard_map(
        functools.partial(shards, mesh.shape["blk"]),
        mesh=mesh, in_specs=in_specs, out_specs=out_specs, check_vma=False,
    )
```
